32 devices in a mesh: space: 8 (over z, x), feat: 4 (over y, core).
Axes of the slice: x: 2, y: 2, z: 4, core: 2. Of those that a mesh axis runs over, the one named last changes fastest.
Arguments:
- bond_state: bfloat16 [16384, 512], P('space', 'feat'), may hold values from -6 to 6
- block_fill: int32 [128], P('space'), may hold values from 64 to 128
- w_in: bfloat16 [512, 512], P(None, 'feat'), may hold values from -0.25 to 0.25
- w_down: bfloat16 [512, 64], P('feat'), may hold values from -0.25 to 0.25
- pair_coef: bfloat16 [896, 128, 128], P('space'), may hold values from -0.5 to 0.5
- pair_source: int32 [896], P('space'), may hold values from 0 to 15
- pair_owner: int32 [896, 1], P('space'), may hold values from 0 to 7; in each aligned block of 112 rows (0 to 111, 112 to 223, ...) at most 16 rows name the same one
- pair_target: int32 [896], P('space'), may hold values from 0 to 15
- w_gate: bfloat16 [64, 512], P(None, 'feat'), may hold values from -0.75 to 0.75
- w_atom_in: bfloat16 [64, 256], P(None, 'feat'), may hold values from -0.75 to 0.75
- atom_state: bfloat16 [256, 4096], P('feat', 'space'), may hold values from -6 to 6
- w_atom: bfloat16 [256, 256], P('feat'), may hold values from -0.375 to 0.375
- bond_ends: int32 [2, 16384], P(None, 'space'), may hold values from 0 to 1535
- w_left: bfloat16 [256, 512], P(None, 'feat'), may hold values from -0.375 to 0.375
- w_right: bfloat16 [256, 512], P(None, 'feat'), may hold values from -0.375 to 0.375
Outputs:
- bond_out: bfloat16 [16384, 512], P('space', 'feat')
- atom_out: bfloat16 [256, 4096], P('feat', 'space')
The draws below stay inside these ranges and needn't reach their ends.
Inputs may be any that keep to these rules, and one draw needn't show every extreme that they name: `pair_owner`: among the 112 pairs of one domain, at most 16 name the same owner, a bound that some block reaches.
All inputs are finite; a program needn't handle non-finite values.
Results may differ from the reference program's by a relative error of at most 0.008.
Values may be sent and summed in bfloat16 or wider, within the bound.
A program may use at most 64 MiB of HBM per device.

```python
import math
import jax
import jax.numpy as jnp
import numpy as np
from jax import lax

DB = 512
DC = 64
DA = 256
BS = 128
BLK_DEV = 16
ATOM_DEV = 512
PAIR_DEV = 112
CAP = 16
NBLK = 128
NBONDS = 16384
NATOMS = 4096
NPAIRS = 896
N_SPACE = 8


def draw_bond_ends(key, part):
    first_key = jax.random.fold_in(key, 11)
    second_key = jax.random.fold_in(key, 23)
    region = jax.random.randint(first_key, (2, NBONDS), 0, 8)
    side = jnp.where(region == 0, 0, jnp.where(region == 7, 2, 1))
    within = jax.random.randint(second_key, (2, NBONDS), 0, ATOM_DEV)
    return (side * ATOM_DEV + within).astype(jnp.int32)


def place_ends(result, key, least, high):
    longest = result.shape.index(max(result.shape))
    spots = []
    for shift in (0, 1):
        where = [jax.random.randint(jax.random.fold_in(key, axis), (), 0, length) for axis, length in enumerate(result.shape)]
        where[longest] = (where[longest] + shift) % result.shape[longest]
        spots.append(tuple(where))
    return result.at[spots[0]].set(least).at[spots[1]].set(high)


def shard_levels(key, shape, pieces, smallest, high):
    factor_of = 1.0
    for dim, blocks in pieces:
        draws = jax.random.uniform(jax.random.fold_in(jax.random.fold_in(key, 6), dim), (blocks,), jnp.float32, smallest / len(pieces), high / len(pieces))
        factor_of = factor_of * jnp.repeat(jnp.exp(draws), shape[dim] // blocks).reshape((-1,) + (1,) * (len(shape) - 1 - dim))
    return factor_of


def shared_out(key, own, number, rows, amount, top, most, slope):
    sequence = jax.random.permutation(key, amount)
    packed, common = shares(amount, rows * top, most, slope, True), shares(amount, rows * top, most, slope, False)
    places = jnp.arange(amount)

    def named(tallies, turn):
        used = int((tallies > 0).sum())
        fixed = max(1, used // 4)
        shifted = fixed + (places - fixed + turn * (used - fixed)) % max(1, amount - fixed)
        return jnp.zeros((amount,), jnp.int32).at[sequence[jnp.where(places < fixed, places, shifted)]].set(jnp.asarray(tallies, jnp.int32))

    tallies = jnp.where(number % 4 == 0, named(packed, number // 4), named(common, number - number // 4 - 1))
    mixed = jax.random.permutation(jax.random.fold_in(own, 3), amount)
    giver, taker = mixed[0:amount // 2 * 2:2], mixed[1:amount // 2 * 2:2]
    margin = jnp.minimum(tallies[giver] - 1, most - tallies[taker]) // 2
    margin = jnp.where((giver == sequence[0]) | (taker == sequence[0]) | (tallies[taker] == 0), 0, jnp.maximum(margin, 0))
    shifted = jax.random.randint(jax.random.fold_in(own, 4), (amount // 2,), 0, 1 << 20) % (margin + 1)
    tallies = tallies.at[giver].add(-shifted).at[taker].add(shifted)
    labels = jnp.searchsorted(jnp.cumsum(tallies), jnp.arange(rows * top), side="right").astype(jnp.int32)
    table = labels.reshape(top, rows).T
    table = table[jax.random.permutation(jax.random.fold_in(own, 1), rows)]
    turn = jax.random.randint(jax.random.fold_in(own, 2), (rows, 1), 0, top)
    return jnp.take_along_axis(table, (jnp.arange(top)[None, :] + turn) % top, axis=1)


def shares(number_of, total, most, skew, full):
    loads = [(1 << 20) // math.isqrt(rank ** skew) + 1 for rank in range(1, number_of + 1)]
    largest = most if full else min(most, max(-(-total // number_of), total * loads[0] // sum(loads)))
    least = 1 if total - largest >= number_of - 1 else 0
    counts, rest = [largest] + [least] * (number_of - 1), total - largest - least * (number_of - 1)
    while rest > 0:
        candidates = [i for i in range(1, number_of) if counts[i] < largest] or [i for i in range(1, number_of) if counts[i] < most]
        pool, left = sum([loads[i] for i in candidates]), rest
        for i in candidates:
            extra = min(most - counts[i], max(1, left * loads[i] // pool), rest)
            counts[i] = counts[i] + extra
            rest = rest - extra
    return np.array(counts)


def centred(key, extent, width, most, shards=(), kind=jnp.bfloat16):
    result = width * jax.random.normal(key, extent, jnp.float32)
    if shards:
        result = result * shard_levels(key, extent, shards, -0.22, 0.18)
    return jnp.clip(result, -most, most).astype(kind)


def setup_inputs(seed: int = 0) -> dict:
    streams_of = jax.random.split(jax.random.key(seed), 16)
    bond_state = centred(streams_of[0], (NBONDS, DB), 1.0, 6.0, ((0, 8), (1, 4)))
    block_fill = place_ends(jax.random.randint(streams_of[1], (NBLK,), BS // 2, BS + 1), jax.random.fold_in(streams_of[1], 1), BS // 2, BS).astype(jnp.int32)
    w_in = centred(streams_of[2], (DB, DB), DB ** -0.5, 0.25, ((1, 4),))
    w_down = centred(streams_of[3], (DB, DC), DB ** -0.5, 0.25, ((0, 4),))
    pair_coef = centred(streams_of[4], (NPAIRS, BS, BS), BS ** -0.5, 0.5, ((0, 8),))
    pair_source = place_ends(jax.random.randint(streams_of[5], (NPAIRS,), 0, BLK_DEV), jax.random.fold_in(streams_of[5], 1), 0, BLK_DEV - 1).astype(jnp.int32)
    pair_owner_keys = jax.random.split(jax.random.fold_in(streams_of[6], 1), NPAIRS // PAIR_DEV)
    pair_owner_turns = jax.random.permutation(jax.random.fold_in(streams_of[6], 3), NPAIRS // PAIR_DEV)
    pair_owner = jax.vmap(lambda own, number: shared_out(jax.random.fold_in(streams_of[6], 2), own, number, PAIR_DEV, N_SPACE, 1, CAP, 2))(pair_owner_keys, pair_owner_turns).reshape((NPAIRS, 1))
    pair_target = place_ends(jax.random.randint(streams_of[7], (NPAIRS,), 0, BLK_DEV), jax.random.fold_in(streams_of[7], 1), 0, BLK_DEV - 1).astype(jnp.int32)
    w_gate = centred(streams_of[8], (DC, DB), DC ** -0.5, 0.75, ((1, 4),))
    w_atom_in = centred(streams_of[9], (DC, DA), DC ** -0.5, 0.75, ((1, 4),))
    atom_state = centred(streams_of[10], (DA, NATOMS), 1.0, 6.0, ((0, 4), (1, 8)))
    w_atom = centred(streams_of[11], (DA, DA), DA ** -0.5, 0.375, ((0, 4),))
    bond_ends = draw_bond_ends(jax.random.fold_in(streams_of[15], 71), 0)
    w_left = centred(streams_of[13], (DA, DB), DA ** -0.5, 0.375, ((1, 4),))
    w_right = centred(streams_of[14], (DA, DB), DA ** -0.5, 0.375, ((1, 4),))
    return dict(bond_state=bond_state, block_fill=block_fill, w_in=w_in, w_down=w_down, pair_coef=pair_coef, pair_source=pair_source, pair_owner=pair_owner, pair_target=pair_target, w_gate=w_gate, w_atom_in=w_atom_in, atom_state=atom_state, w_atom=w_atom, bond_ends=bond_ends, w_left=w_left, w_right=w_right)


def reference(bond_state, block_fill, w_in, w_down, pair_coef, pair_source, pair_owner, pair_target, w_gate, w_atom_in, atom_state, w_atom, bond_ends, w_left, w_right):
    bond_count = bond_state.shape[0]
    block_count = block_fill.shape[0]
    atom_count = atom_state.shape[1]
    position = jnp.arange(BS, dtype=jnp.int32)[None, :]
    real_mask = (position < block_fill[:, None]).astype(jnp.float32).reshape(bond_count)
    hidden = jax.nn.silu(jnp.dot(bond_state, w_in, preferred_element_type=jnp.float32)).astype(jnp.bfloat16)
    angular = (jnp.dot(hidden, w_down, preferred_element_type=jnp.float32) * real_mask[:, None]).astype(jnp.bfloat16)
    angular_blocks = angular.reshape(block_count, BS, DC)
    pair_device = jnp.arange(NPAIRS, dtype=jnp.int32) // PAIR_DEV
    source_ids = (pair_device * BLK_DEV + pair_source).astype(jnp.int32)
    target_ids = (pair_owner[:, 0] * BLK_DEV + pair_target).astype(jnp.int32)

    def one_device(running, device):
        first_pair = (device * PAIR_DEV).astype(jnp.int32)
        own_sources = lax.dynamic_slice_in_dim(source_ids, first_pair, PAIR_DEV)
        own_targets = lax.dynamic_slice_in_dim(target_ids, first_pair, PAIR_DEV)
        coefficients = lax.dynamic_slice_in_dim(pair_coef, first_pair, PAIR_DEV, 0).astype(jnp.float32)
        gathered = angular_blocks[own_sources].astype(jnp.float32)
        contrib = jnp.einsum("pij,pjc->pic", coefficients, gathered)
        rounded = lax.optimization_barrier(contrib.astype(jnp.bfloat16)).astype(jnp.float32)
        return running.at[own_targets].add(rounded), None

    start_sum = jnp.zeros((block_count, BS, DC), jnp.float32)
    block_sums, unused = lax.scan(one_device, start_sum, jnp.arange(N_SPACE, dtype=jnp.int32))
    message = (block_sums.reshape(bond_count, DC) * real_mask[:, None]).astype(jnp.bfloat16)
    gate_pre = jnp.dot(message, w_gate, preferred_element_type=jnp.float32)
    to_atoms = jnp.dot(message, w_atom_in, preferred_element_type=jnp.float32)
    bond_device = jnp.arange(bond_count, dtype=jnp.int32) // (BLK_DEV * BS)
    window_base = bond_device * ATOM_DEV - ATOM_DEV
    left_atoms = ((window_base + bond_ends[0]) % atom_count).astype(jnp.int32)
    right_atoms = ((window_base + bond_ends[1]) % atom_count).astype(jnp.int32)
    atom_sums = jax.ops.segment_sum(to_atoms, right_atoms, num_segments=atom_count)
    atom_counts = jax.ops.segment_sum(real_mask, right_atoms, num_segments=atom_count)
    mean_in = (atom_sums / jnp.maximum(atom_counts, 1.0)[:, None]).astype(jnp.bfloat16)
    atom_pre = jnp.dot(mean_in, w_atom, preferred_element_type=jnp.float32)
    atom_new = (atom_state.T.astype(jnp.float32) + jax.nn.silu(atom_pre)).astype(jnp.bfloat16)
    mixed_atoms = jnp.dot(atom_new[left_atoms], w_left, preferred_element_type=jnp.float32) + jnp.dot(atom_new[right_atoms], w_right, preferred_element_type=jnp.float32)
    update = jax.nn.sigmoid(gate_pre) * (hidden.astype(jnp.float32) + jax.nn.silu(mixed_atoms))
    bond_out = (bond_state.astype(jnp.float32) + real_mask[:, None] * update).astype(jnp.bfloat16)
    return bond_out, atom_new.T
```

```python
import functools

import jax
import jax.numpy as jnp
from jax import lax
from jax.experimental import pallas as pl
from jax.experimental.pallas import tpu as pltpu
from jax.sharding import PartitionSpec as P


def passed_along(value, axis, steps):
    count = lax.axis_size(axis)
    pairs = [(source, (source + steps) % count) for source in range(count)]
    return lax.ppermute(value, axis, pairs)


def extended(cells, sides, width):
    for axis, dim in sides:
        count = lax.axis_size(axis)
        head = lax.slice_in_dim(cells, 0, width, axis=dim)
        tail = lax.slice_in_dim(cells, cells.shape[dim] - width, cells.shape[dim], axis=dim)
        cells = jnp.concatenate(
            [
                lax.ppermute(tail, axis, [(i, (i + 1) % count) for i in range(count)]),
                cells,
                lax.ppermute(head, axis, [((i + 1) % count, i) for i in range(count)]),
            ],
            axis=dim,
        )
    return cells


def local(
    bond_state,
    block_fill,
    w_in,
    w_down,
    pair_coef,
    pair_source,
    pair_owner,
    pair_target,
    w_gate,
    w_atom_in,
    atom_state,
    w_atom,
    bond_ends,
    w_left,
    w_right,
):
    bond_slots = bond_state.shape[0]
    blocks = block_fill.shape[0]
    block_size = bond_slots // blocks
    pair_count = pair_source.shape[0]
    spaces = lax.axis_size("space")
    feat_count = lax.axis_size("feat")
    capacity = max(2, min(blocks, 2 * pair_count // spaces))
    channels = w_down.shape[1]
    own_channels = channels // feat_count
    atom_cols = atom_state.shape[1]
    contract_first = (((0,), (0,)), ((), ()))
    position = lax.broadcasted_iota(jnp.int32, (blocks, block_size), 1)
    real_mask = (position < block_fill[:, None]).astype(jnp.float32).reshape(bond_slots)
    full_rows = lax.all_gather(bond_state, "feat", axis=1, tiled=True)
    whole_in, whole_down = (
        lax.all_gather(w_in, "feat", axis=1, tiled=True),
        lax.all_gather(w_down, "feat", axis=0, tiled=True),
    )
    all_hidden = jax.nn.silu(
        jnp.dot(full_rows, whole_in, preferred_element_type=jnp.float32)
    ).astype(jnp.bfloat16)
    own_units = w_in.shape[1]
    hidden = lax.dynamic_slice_in_dim(all_hidden, lax.axis_index("feat") * own_units, own_units, 1)
    down_columns = lax.dynamic_slice_in_dim(
        whole_down, lax.axis_index("feat") * own_channels, own_channels, 1
    )
    angular_sum = lax.dot_general(
        down_columns, all_hidden, (((0,), (1,)), ((), ())), preferred_element_type=jnp.float32
    )
    angular = (angular_sum * real_mask[None, :]).astype(jnp.bfloat16)
    angular_blocks = angular.reshape(own_channels, blocks, block_size)
    sources = jnp.take(angular_blocks, pair_source, axis=1)
    contrib = jnp.einsum(
        "cpj,pij->pci", sources, pair_coef, preferred_element_type=jnp.float32
    ).astype(jnp.bfloat16)
    owner_ids = pair_owner[:, 0]
    owner_table = (
        owner_ids[:, None] == lax.broadcasted_iota(jnp.int32, (pair_count, spaces), 1)
    ).astype(jnp.int32)
    slot_rank = jnp.sum(jnp.cumsum(owner_table, axis=0) * owner_table, axis=1) - 1
    flat_slot = owner_ids * capacity + slot_rank
    outgoing = (
        jnp.zeros((spaces * capacity, own_channels, block_size), jnp.bfloat16)
        .at[flat_slot]
        .set(contrib)
    )
    labels = jnp.full((spaces * capacity,), blocks, jnp.int32).at[flat_slot].set(pair_target)
    incoming, arrived = (
        lax.all_to_all(
            outgoing.reshape(spaces, capacity, own_channels, block_size),
            "space",
            split_axis=0,
            concat_axis=0,
            tiled=True,
        ),
        lax.all_to_all(
            labels.reshape(spaces, capacity), "space", split_axis=0, concat_axis=0, tiled=True
        ),
    )
    chooser = (
        arrived.reshape(spaces * capacity)[None, :]
        == lax.broadcasted_iota(jnp.int32, (blocks, spaces * capacity), 0)
    ).astype(jnp.bfloat16)
    block_sums = jnp.einsum(
        "kq,qcr->ckr",
        chooser,
        incoming.reshape(spaces * capacity, own_channels, block_size),
        preferred_element_type=jnp.float32,
    )
    message = (block_sums.reshape(own_channels, bond_slots) * real_mask[None, :]).astype(
        jnp.bfloat16
    )
    shard_piece = lax.all_gather(message, "feat", axis=0, tiled=True)
    gate_pre = lax.dot_general(
        shard_piece, w_gate, contract_first, preferred_element_type=jnp.float32
    )
    to_atoms = lax.dot_general(
        shard_piece, w_atom_in, contract_first, preferred_element_type=jnp.float32
    )
    window = 3 * atom_cols
    window_sums = jax.ops.segment_sum(to_atoms, bond_ends[1], num_segments=window).T
    window_counts = jax.ops.segment_sum(real_mask, bond_ends[1], num_segments=window)
    from_upper = (
        passed_along(window_sums[:, :atom_cols].astype(jnp.bfloat16), "space", -1).astype(
            jnp.float32
        ),
        passed_along(window_counts[:atom_cols].astype(jnp.bfloat16), "space", -1).astype(
            jnp.float32
        ),
    )
    from_lower = (
        passed_along(window_sums[:, 2 * atom_cols :].astype(jnp.bfloat16), "space", 1).astype(
            jnp.float32
        ),
        passed_along(window_counts[2 * atom_cols :].astype(jnp.bfloat16), "space", 1).astype(
            jnp.float32
        ),
    )
    atom_sums = window_sums[:, atom_cols : 2 * atom_cols] + from_upper[0] + from_lower[0]
    atom_counts = window_counts[atom_cols : 2 * atom_cols] + from_upper[1] + from_lower[1]
    mean_in = (atom_sums / jnp.maximum(atom_counts, 1.0)[None, :]).astype(jnp.bfloat16)
    partial_pre = lax.dot_general(
        w_atom, mean_in, contract_first, preferred_element_type=jnp.float32
    )
    own_pre = lax.psum_scatter(
        partial_pre.astype(jnp.bfloat16), "feat", scatter_dimension=0, tiled=True
    ).astype(jnp.float32)
    atom_out = (atom_state + jax.nn.silu(own_pre)).astype(jnp.bfloat16)
    own_window = extended(atom_out, (("space", 1),), atom_cols)
    neighbours = lax.all_gather(own_window, "feat", axis=0, tiled=True)
    left_rows = jnp.take(neighbours, bond_ends[0], axis=1)
    right_rows = jnp.take(neighbours, bond_ends[1], axis=1)
    mixed_atoms = lax.dot_general(
        left_rows, w_left, contract_first, preferred_element_type=jnp.float32
    ) + lax.dot_general(right_rows, w_right, contract_first, preferred_element_type=jnp.float32)
    update = jax.nn.sigmoid(gate_pre) * (hidden.astype(jnp.float32) + jax.nn.silu(mixed_atoms))
    bond_out = (bond_state + real_mask[:, None] * update).astype(jnp.bfloat16)
    return (bond_out, atom_out)


MESH_IDS = pl.DeviceIdType.MESH


def silu(value):
    return value / (1.0 + jnp.exp(-value))


def greet(peers):
    barrier = pltpu.get_barrier_semaphore()
    for peer in peers:
        pl.semaphore_signal(barrier, inc=1, device_id=peer, device_id_type=MESH_IDS)
    pl.semaphore_wait(barrier, len(peers))


def remote(source, target, sends, receives, number, peer):
    return pltpu.make_async_remote_copy(
        src_ref=source,
        dst_ref=target,
        send_sem=sends.at[number],
        recv_sem=receives.at[number],
        device_id=peer,
        device_id_type=MESH_IDS,
    )


def feat_peers(count):
    space, feat = lax.axis_index("space"), lax.axis_index("feat")
    return [(space, lax.rem(feat + step, count)) for step in range(1, count)]


def down(value, step):
    count = lax.axis_size("space")
    return lax.rem(value + step + count, count)


def bond_kernel(
    feats,
    fill,
    bond,
    w_in,
    w_down,
    state,
    angular,
    hidden,
    state_window,
    rows,
    whole_in,
    whole_down,
    angular_rows,
    sends,
    receives,
):
    space, feat = lax.axis_index("space"), lax.axis_index("feat")
    share = bond.shape[0] // feats
    width, units = bond.shape[1], w_in.shape[1]
    own_channels = angular.shape[0]
    atoms = state.shape[1]
    block_size = bond.shape[0] // fill.shape[0]
    peers = feat_peers(feats)
    lower, upper = (down(space, -1), feat), (down(space, 1), feat)
    greet(peers + [lower, upper])
    own_width = pl.ds(pl.multiple_of(feat * width, width), width)
    own_units = pl.ds(pl.multiple_of(feat * units, units), units)
    copies, late = [], []
    number = 0
    for peer in peers:
        their_rows = pl.ds(pl.multiple_of(peer[1] * share, share), share)
        copies.append(remote(w_in, whole_in.at[:, own_units], sends, receives, number, peer))
        copies.append(
            remote(bond.at[their_rows], rows.at[:, own_width], sends, receives, number + 1, peer)
        )
        copies.append(remote(w_down, whole_down.at[own_units], sends, receives, number + 2, peer))
        number += 3
    late.append(
        remote(state, state_window.at[:, 2 * atoms :], sends, receives, number, lower)
    )
    late.append(
        remote(state, state_window.at[:, :atoms], sends, receives, number + 1, upper)
    )
    number += 2
    for copy in copies + late:
        copy.start()
    own_rows = pl.ds(pl.multiple_of(feat * share, share), share)
    rows[:, own_width] = bond[own_rows]
    whole_in[:, own_units] = w_in[...]
    whole_down[own_units] = w_down[...]
    state_window[:, atoms : 2 * atoms] = state[...]
    for copy in copies:
        copy.wait()
    hidden[...] = silu(
        jnp.dot(rows[...], whole_in[...], preferred_element_type=jnp.float32)
    ).astype(jnp.bfloat16)
    sums = lax.dot_general(
        whole_down[...], hidden[...], (((0,), (1,)), ((), ())), preferred_element_type=jnp.float32
    )
    for part in range(share // block_size):
        limit = fill[feat * (share // block_size) + part]
        place = lax.broadcasted_iota(jnp.int32, (1, block_size), 1)
        mask = jnp.where(place < limit, 1.0, 0.0)
        span = slice(part * block_size, (part + 1) * block_size)
        angular_rows[:, span] = (sums[:, span] * mask).astype(jnp.bfloat16)
    own_span = pl.ds(pl.multiple_of(feat * share, share), share)
    back = []
    for peer in peers:
        theirs = pl.ds(pl.multiple_of(peer[1] * own_channels, own_channels), own_channels)
        back.append(
            remote(
                angular_rows.at[theirs], angular.at[:, own_span], sends, receives, number, peer
            )
        )
        number += 1
    for copy in back:
        copy.start()
    mine = pl.ds(pl.multiple_of(feat * own_channels, own_channels), own_channels)
    angular[:, own_span] = angular_rows[mine]
    for copy in back + late:
        copy.wait()


def pair_kernel(steps, blocks, source, owner, target, angular, coefficients, outgoing, total):
    step = pl.program_id(0)
    count = coefficients.shape[0]
    block_size = coefficients.shape[1]
    group = 14 if count % 14 == 0 else 1

    @pl.when(step == 0)
    def clear():
        total[...] = jnp.zeros_like(total)

    def several(turn, carry):
        products = []
        for offset in range(group):
            place = turn * group + offset
            start = pl.multiple_of(source[step * count + place] * block_size, block_size)
            products.append(
                lax.dot_general(
                    angular[:, pl.ds(start, block_size)],
                    coefficients[place],
                    (((1,), (1,)), ((), ())),
                    preferred_element_type=jnp.float32,
                )
            )
        for offset in range(group):
            pair = step * count + turn * group + offset
            slot = owner[pair] * blocks + target[pair]
            total[slot] += products[offset]
        return carry

    lax.fori_loop(0, count // group, several, 0)

    @pl.when(step == steps - 1)
    def finish():
        outgoing[...] = total[...].astype(jnp.bfloat16)


def update_kernel(
    spaces,
    feats,
    fill,
    outgoing,
    hidden_rows,
    state_window,
    bond,
    ends,
    w_gate,
    w_atom_in,
    w_atom,
    w_left,
    w_right,
    bond_out,
    atom_out,
    incoming,
    left_hot,
    right_hot,
    summed,
    message,
    halo_out,
    halo_in,
    mean,
    means,
    states,
    whole_atom_in,
    whole_atom,
    hidden,
    window_atoms,
    space_sends,
    space_receives,
    sends,
    receives,
):
    space, feat = lax.axis_index("space"), lax.axis_index("feat")
    blocks = fill.shape[0]
    slots = bond.shape[0]
    size = slots // blocks
    channels = summed.shape[0] // 2
    width = bond.shape[1]
    share = slots // feats
    window = state_window.shape[1]
    atoms = window // 3
    inner = w_atom.shape[0]
    peers = feat_peers(feats)
    lower, upper = down(space, -1), down(space, 1)
    sides = [(lower, feat), (upper, feat)]
    diagonal = [(side, peer[1]) for side in (lower, upper) for peer in peers]
    far = [(down(space, step), feat) for step in range(2, spaces - 1)]
    greet(peers + sides + diagonal + far)
    crossing = []
    for step in range(1, spaces):
        goal = down(space, step)
        crossing.append(
            remote(
                outgoing.at[pl.ds(goal * blocks, blocks)],
                incoming.at[space],
                space_sends,
                space_receives,
                step,
                (goal, feat),
            )
        )
    for copy in crossing:
        copy.start()
    own_inner = pl.ds(pl.multiple_of(feat * inner, inner), inner)
    own_span = pl.ds(pl.multiple_of(feat * share, share), share)
    weights, returned = [], []
    number = 0
    for peer in peers:
        theirs = pl.ds(pl.multiple_of(peer[1] * width, width), width)
        weights.append(
            remote(w_atom_in, whole_atom_in.at[feat], sends, receives, number, peer)
        )
        weights.append(remote(w_atom, whole_atom.at[own_inner], sends, receives, number + 1, peer))
        weights.append(
            remote(state_window, states.at[own_inner], sends, receives, number + 2, peer)
        )
        returned.append(
            remote(
                hidden_rows.at[:, theirs], hidden.at[own_span], sends, receives, number + 3, peer
            )
        )
        number += 4
    for copy in weights + returned:
        copy.start()
    incoming[space] = outgoing[pl.ds(space * blocks, blocks)]
    whole_atom_in[feat] = w_atom_in[...]
    whole_atom[own_inner] = w_atom[...]
    states[own_inner] = state_window[...]
    hidden[own_span] = hidden_rows[:, pl.ds(pl.multiple_of(feat * width, width), width)]
    place = lax.broadcasted_iota(jnp.int32, (size, window), 1)

    def spread(block, carry):
        span = pl.ds(pl.multiple_of(block * size, size), size)
        pair = ends[span]
        left_hot[span] = jnp.where(place == pair[:, 0:1], 1.0, 0.0).astype(jnp.bfloat16)
        right_hot[span] = jnp.where(place == pair[:, 1:2], 1.0, 0.0).astype(jnp.bfloat16)
        return carry

    lax.fori_loop(0, blocks, spread, 0)
    for copy in crossing:
        copy.wait()
    own_channels = pl.ds(pl.multiple_of(feat * channels, channels), channels)
    for block in range(blocks):
        span = slice(block * size, (block + 1) * size)
        total = incoming[0, block].astype(jnp.float32)
        for source in range(1, spaces):
            total = total + incoming[source, block].astype(jnp.float32)
        lane = lax.broadcasted_iota(jnp.int32, (channels, size), 1)
        mask = jnp.where(lane < fill[block], 1.0, 0.0)
        summed[:channels, span] = (total * mask).astype(jnp.bfloat16)
        summed[channels:, span] = mask.astype(jnp.bfloat16)
    message[own_channels] = summed[:channels]
    spreading = []
    for peer in peers:
        spreading.append(
            remote(
                summed.at[:channels], message.at[own_channels], sends, receives, number, peer
            )
        )
        number += 1
    partial = jnp.dot(summed[...], right_hot[...], preferred_element_type=jnp.float32)
    halo_out[0] = partial[:, :atoms]
    halo_out[1] = partial[:, 2 * atoms :]
    halos = [
        remote(halo_out.at[0], halo_in.at[0], sends, receives, number, sides[0]),
        remote(halo_out.at[1], halo_in.at[1], sends, receives, number + 1, sides[1]),
    ]
    number += 2
    for copy in halos + spreading:
        copy.start()
    for copy in halos:
        copy.wait()
    full = partial[:, atoms : 2 * atoms] + halo_in[0] + halo_in[1]
    mean[...] = (full[:channels] / jnp.maximum(full[channels:], 1.0)).astype(jnp.bfloat16)
    sharing = []
    for peer in peers:
        spot = means.at[own_channels, atoms : 2 * atoms]
        sharing.append(remote(mean, spot, sends, receives, number, peer))
        number += 1
    for near in range(feats):
        for side in range(2):
            peer = ((lower, upper)[side], lax.rem(feat + near, feats))
            columns = slice(2 * atoms, 3 * atoms) if side == 0 else slice(0, atoms)
            spot = means.at[own_channels, columns]
            sharing.append(remote(mean, spot, sends, receives, number, peer))
            number += 1
    for copy in sharing:
        copy.start()
    means[own_channels, atoms : 2 * atoms] = mean[...]
    for copy in sharing + weights:
        copy.wait()
    first = (((0,), (0,)), ((), ()))
    last = (((1,), (1,)), ((), ()))
    mean_in = jnp.concatenate(
        [
            lax.dot_general(
                whole_atom_in[near], means[...], first, preferred_element_type=jnp.float32
            ).astype(jnp.bfloat16)
            for near in range(feats)
        ],
        axis=0,
    )
    pre = lax.dot_general(whole_atom[...], mean_in, first, preferred_element_type=jnp.float32)
    window_atoms[...] = (states[...].astype(jnp.float32) + silu(pre)).astype(jnp.bfloat16)
    atom_out[...] = window_atoms[own_inner, atoms : 2 * atoms]
    for copy in spreading + returned:
        copy.wait()
    row = lax.broadcasted_iota(jnp.int32, (size, width), 0)

    def finish(block, carry):
        span = pl.ds(pl.multiple_of(block * size, size), size)
        left = lax.dot_general(
            left_hot[span], window_atoms[...], last, preferred_element_type=jnp.float32
        ).astype(jnp.bfloat16)
        right = lax.dot_general(
            right_hot[span], window_atoms[...], last, preferred_element_type=jnp.float32
        ).astype(jnp.bfloat16)
        mixed = jnp.dot(left, w_left[...], preferred_element_type=jnp.float32) + jnp.dot(
            right, w_right[...], preferred_element_type=jnp.float32
        )
        gate = lax.dot_general(
            message[:, span], w_gate[...], first, preferred_element_type=jnp.float32
        )
        update = (hidden[span].astype(jnp.float32) + silu(mixed)) / (1.0 + jnp.exp(-gate))
        old = bond[span].astype(jnp.float32)
        bond_out[span] = (old + jnp.where(row < fill[block], update, 0.0)).astype(jnp.bfloat16)
        return carry

    lax.fori_loop(0, blocks, finish, 0)


def fast(
    bond_state,
    block_fill,
    w_in,
    w_down,
    pair_coef,
    pair_source,
    pair_owner,
    pair_target,
    w_gate,
    w_atom_in,
    atom_state,
    w_atom,
    bond_ends,
    w_left,
    w_right,
):
    spaces, feats = lax.axis_size("space"), lax.axis_size("feat")
    slots, width = bond_state.shape
    blocks = block_fill.shape[0]
    size = slots // blocks
    pairs = pair_source.shape[0]
    features, units = w_in.shape
    channels = w_down.shape[1]
    own_channels = channels // feats
    share = slots // feats
    inner, atoms = atom_state.shape
    half, single = jnp.bfloat16, jnp.float32
    vmem = pl.BlockSpec(memory_space=pltpu.VMEM)
    smem = pl.BlockSpec(memory_space=pltpu.SMEM)
    dma = pltpu.SemaphoreType.DMA
    first_copies = 4 * (feats - 1) + 2
    angular, hidden_rows, state_window = pl.pallas_call(
        functools.partial(bond_kernel, feats),
        out_shape=(
            jax.ShapeDtypeStruct((own_channels, slots), half),
            jax.ShapeDtypeStruct((share, units * feats), half),
            jax.ShapeDtypeStruct((inner, 3 * atoms), half),
        ),
        in_specs=[smem] + [vmem] * 4,
        out_specs=(vmem, vmem, vmem),
        scratch_shapes=[
            pltpu.VMEM((share, features), half),
            pltpu.VMEM((features, units * feats), half),
            pltpu.VMEM((features, channels), half),
            pltpu.VMEM((channels, share), half),
            dma((first_copies,)),
            dma((first_copies,)),
        ],
        compiler_params=pltpu.CompilerParams(collective_id=0, has_side_effects=True),
        name="bond_mlp",
    )(block_fill, bond_state, w_in, w_down, atom_state)
    steps = 4 if pairs % 4 == 0 else 1
    part = pairs // steps
    outgoing = pl.pallas_call(
        functools.partial(pair_kernel, steps, blocks),
        grid=(steps,),
        out_shape=jax.ShapeDtypeStruct((spaces * blocks, own_channels, size), half),
        in_specs=[
            smem,
            smem,
            smem,
            pl.BlockSpec((own_channels, slots), lambda i: (0, 0)),
            pl.BlockSpec((part, size, size), lambda i: (i, 0, 0)),
        ],
        out_specs=pl.BlockSpec((spaces * blocks, own_channels, size), lambda i: (0, 0, 0)),
        scratch_shapes=[pltpu.VMEM((spaces * blocks, own_channels, size), single)],
        name="pair_sums",
    )(pair_source, pair_owner.reshape(pairs), pair_target, angular, pair_coef)
    last_copies = 4 * (feats - 1) + (feats - 1) + 2 + (feats - 1) + 2 * feats
    bond_out, atom_out = pl.pallas_call(
        functools.partial(update_kernel, spaces, feats),
        out_shape=(
            jax.ShapeDtypeStruct((slots, width), half),
            jax.ShapeDtypeStruct((inner, atoms), half),
        ),
        in_specs=[smem] + [vmem] * 10,
        out_specs=(vmem, vmem),
        scratch_shapes=[
            pltpu.VMEM((spaces, blocks, own_channels, size), half),
            pltpu.VMEM((slots, 3 * atoms), half),
            pltpu.VMEM((slots, 3 * atoms), half),
            pltpu.VMEM((2 * own_channels, slots), half),
            pltpu.VMEM((channels, slots), half),
            pltpu.VMEM((2, 2 * own_channels, atoms), single),
            pltpu.VMEM((2, 2 * own_channels, atoms), single),
            pltpu.VMEM((own_channels, atoms), half),
            pltpu.VMEM((channels, 3 * atoms), half),
            pltpu.VMEM((inner * feats, 3 * atoms), half),
            pltpu.VMEM((feats,) + w_atom_in.shape, half),
            pltpu.VMEM((inner * feats, w_atom.shape[1]), half),
            pltpu.VMEM((slots, width), half),
            pltpu.VMEM((inner * feats, 3 * atoms), half),
            dma((spaces,)),
            dma((spaces,)),
            dma((last_copies,)),
            dma((last_copies,)),
        ],
        compiler_params=pltpu.CompilerParams(
            collective_id=1, has_side_effects=True, vmem_limit_bytes=60 * 2**20
        ),
        name="bond_update",
    )(
        block_fill,
        outgoing,
        hidden_rows,
        state_window,
        bond_state,
        bond_ends.T,
        w_gate,
        w_atom_in,
        w_atom,
        w_left,
        w_right,
    )
    return (bond_out, atom_out)


def solution(mesh):
    placed = (
        P("space", "feat"),
        P("space"),
        P(None, "feat"),
        P("feat", None),
        P("space", None, None),
        P("space"),
        P("space", None),
        P("space"),
        P(None, "feat"),
        P(None, "feat"),
        P("feat", "space"),
        P("feat", None),
        P(None, "space"),
        P(None, "feat"),
        P(None, "feat"),
    )
    spaces = mesh.shape["space"]
    body = fast if 4 <= spaces <= 16 else local
    return jax.shard_map(
        body,
        mesh=mesh,
        in_specs=placed,
        out_specs=(P("space", "feat"), P("feat", "space")),
        check_vma=False,
    )
```

```python
import functools

import jax
import jax.numpy as jnp
from jax import lax
from jax.experimental import pallas as pl
from jax.experimental.pallas import tpu as pltpu
from jax.sharding import PartitionSpec as P


def passed_along(value, axis, steps):
    count = lax.axis_size(axis)
    pairs = [(source, (source + steps) % count) for source in range(count)]
    return lax.ppermute(value, axis, pairs)


def extended(cells, sides, width):
    for axis, dim in sides:
        count = lax.axis_size(axis)
        head = lax.slice_in_dim(cells, 0, width, axis=dim)
        tail = lax.slice_in_dim(cells, cells.shape[dim] - width, cells.shape[dim], axis=dim)
        cells = jnp.concatenate(
            [
                lax.ppermute(tail, axis, [(i, (i + 1) % count) for i in range(count)]),
                cells,
                lax.ppermute(head, axis, [((i + 1) % count, i) for i in range(count)]),
            ],
            axis=dim,
        )
    return cells


def local(
    bond_state,
    block_fill,
    w_in,
    w_down,
    pair_coef,
    pair_source,
    pair_owner,
    pair_target,
    w_gate,
    w_atom_in,
    atom_state,
    w_atom,
    bond_ends,
    w_left,
    w_right,
):
    bond_slots = bond_state.shape[0]
    blocks = block_fill.shape[0]
    block_size = bond_slots // blocks
    pair_count = pair_source.shape[0]
    spaces = lax.axis_size("space")
    feat_count = lax.axis_size("feat")
    capacity = max(2, min(blocks, 2 * pair_count // spaces))
    channels = w_down.shape[1]
    own_channels = channels // feat_count
    atom_cols = atom_state.shape[1]
    contract_first = (((0,), (0,)), ((), ()))
    position = lax.broadcasted_iota(jnp.int32, (blocks, block_size), 1)
    real_mask = (position < block_fill[:, None]).astype(jnp.float32).reshape(bond_slots)
    full_rows = lax.all_gather(bond_state, "feat", axis=1, tiled=True)
    whole_in, whole_down = (
        lax.all_gather(w_in, "feat", axis=1, tiled=True),
        lax.all_gather(w_down, "feat", axis=0, tiled=True),
    )
    all_hidden = jax.nn.silu(
        jnp.dot(full_rows, whole_in, preferred_element_type=jnp.float32)
    ).astype(jnp.bfloat16)
    own_units = w_in.shape[1]
    hidden = lax.dynamic_slice_in_dim(all_hidden, lax.axis_index("feat") * own_units, own_units, 1)
    down_columns = lax.dynamic_slice_in_dim(
        whole_down, lax.axis_index("feat") * own_channels, own_channels, 1
    )
    angular_sum = lax.dot_general(
        down_columns, all_hidden, (((0,), (1,)), ((), ())), preferred_element_type=jnp.float32
    )
    angular = (angular_sum * real_mask[None, :]).astype(jnp.bfloat16)
    angular_blocks = angular.reshape(own_channels, blocks, block_size)
    sources = jnp.take(angular_blocks, pair_source, axis=1)
    contrib = jnp.einsum(
        "cpj,pij->pci", sources, pair_coef, preferred_element_type=jnp.float32
    ).astype(jnp.bfloat16)
    owner_ids = pair_owner[:, 0]
    owner_table = (
        owner_ids[:, None] == lax.broadcasted_iota(jnp.int32, (pair_count, spaces), 1)
    ).astype(jnp.int32)
    slot_rank = jnp.sum(jnp.cumsum(owner_table, axis=0) * owner_table, axis=1) - 1
    flat_slot = owner_ids * capacity + slot_rank
    outgoing = (
        jnp.zeros((spaces * capacity, own_channels, block_size), jnp.bfloat16)
        .at[flat_slot]
        .set(contrib)
    )
    labels = jnp.full((spaces * capacity,), blocks, jnp.int32).at[flat_slot].set(pair_target)
    incoming, arrived = (
        lax.all_to_all(
            outgoing.reshape(spaces, capacity, own_channels, block_size),
            "space",
            split_axis=0,
            concat_axis=0,
            tiled=True,
        ),
        lax.all_to_all(
            labels.reshape(spaces, capacity), "space", split_axis=0, concat_axis=0, tiled=True
        ),
    )
    chooser = (
        arrived.reshape(spaces * capacity)[None, :]
        == lax.broadcasted_iota(jnp.int32, (blocks, spaces * capacity), 0)
    ).astype(jnp.bfloat16)
    block_sums = jnp.einsum(
        "kq,qcr->ckr",
        chooser,
        incoming.reshape(spaces * capacity, own_channels, block_size),
        preferred_element_type=jnp.float32,
    )
    message = (block_sums.reshape(own_channels, bond_slots) * real_mask[None, :]).astype(
        jnp.bfloat16
    )
    shard_piece = lax.all_gather(message, "feat", axis=0, tiled=True)
    gate_pre = lax.dot_general(
        shard_piece, w_gate, contract_first, preferred_element_type=jnp.float32
    )
    to_atoms = lax.dot_general(
        shard_piece, w_atom_in, contract_first, preferred_element_type=jnp.float32
    )
    window = 3 * atom_cols
    window_sums = jax.ops.segment_sum(to_atoms, bond_ends[1], num_segments=window).T
    window_counts = jax.ops.segment_sum(real_mask, bond_ends[1], num_segments=window)
    from_upper = (
        passed_along(window_sums[:, :atom_cols].astype(jnp.bfloat16), "space", -1).astype(
            jnp.float32
        ),
        passed_along(window_counts[:atom_cols].astype(jnp.bfloat16), "space", -1).astype(
            jnp.float32
        ),
    )
    from_lower = (
        passed_along(window_sums[:, 2 * atom_cols :].astype(jnp.bfloat16), "space", 1).astype(
            jnp.float32
        ),
        passed_along(window_counts[2 * atom_cols :].astype(jnp.bfloat16), "space", 1).astype(
            jnp.float32
        ),
    )
    atom_sums = window_sums[:, atom_cols : 2 * atom_cols] + from_upper[0] + from_lower[0]
    atom_counts = window_counts[atom_cols : 2 * atom_cols] + from_upper[1] + from_lower[1]
    mean_in = (atom_sums / jnp.maximum(atom_counts, 1.0)[None, :]).astype(jnp.bfloat16)
    partial_pre = lax.dot_general(
        w_atom, mean_in, contract_first, preferred_element_type=jnp.float32
    )
    own_pre = lax.psum_scatter(
        partial_pre.astype(jnp.bfloat16), "feat", scatter_dimension=0, tiled=True
    ).astype(jnp.float32)
    atom_out = (atom_state + jax.nn.silu(own_pre)).astype(jnp.bfloat16)
    own_window = extended(atom_out, (("space", 1),), atom_cols)
    neighbours = lax.all_gather(own_window, "feat", axis=0, tiled=True)
    left_rows = jnp.take(neighbours, bond_ends[0], axis=1)
    right_rows = jnp.take(neighbours, bond_ends[1], axis=1)
    mixed_atoms = lax.dot_general(
        left_rows, w_left, contract_first, preferred_element_type=jnp.float32
    ) + lax.dot_general(right_rows, w_right, contract_first, preferred_element_type=jnp.float32)
    update = jax.nn.sigmoid(gate_pre) * (hidden.astype(jnp.float32) + jax.nn.silu(mixed_atoms))
    bond_out = (bond_state + real_mask[:, None] * update).astype(jnp.bfloat16)
    return (bond_out, atom_out)


MESH_IDS = pl.DeviceIdType.MESH


def silu(value):
    return value / (1.0 + jnp.exp(-value))


def greet(peers):
    barrier = pltpu.get_barrier_semaphore()
    for peer in peers:
        pl.semaphore_signal(barrier, inc=1, device_id=peer, device_id_type=MESH_IDS)
    pl.semaphore_wait(barrier, len(peers))


def remote(source, target, sends, receives, number, peer):
    return pltpu.make_async_remote_copy(
        src_ref=source,
        dst_ref=target,
        send_sem=sends.at[number],
        recv_sem=receives.at[number],
        device_id=peer,
        device_id_type=MESH_IDS,
    )


def feat_peers(count):
    space, feat = lax.axis_index("space"), lax.axis_index("feat")
    return [(space, lax.rem(feat + step, count)) for step in range(1, count)]


def down(value, step):
    count = lax.axis_size("space")
    return lax.rem(value + step + count, count)


def bond_kernel(
    feats,
    fill,
    bond,
    w_in,
    w_down,
    state,
    angular,
    hidden,
    state_window,
    rows,
    whole_in,
    whole_down,
    angular_rows,
    sends,
    receives,
):
    space, feat = lax.axis_index("space"), lax.axis_index("feat")
    share = bond.shape[0] // feats
    width, units = bond.shape[1], w_in.shape[1]
    own_channels = angular.shape[0]
    atoms = state.shape[1]
    block_size = bond.shape[0] // fill.shape[0]
    peers = feat_peers(feats)
    lower, upper = (down(space, -1), feat), (down(space, 1), feat)
    greet(peers + [lower, upper])
    own_width = pl.ds(pl.multiple_of(feat * width, width), width)
    own_units = pl.ds(pl.multiple_of(feat * units, units), units)
    copies, late = [], []
    number = 0
    relayed = feats == 4
    if relayed:
        partner = (space, feat + 1 - 2 * lax.rem(feat, 2))
        opposite = (space, lax.rem(feat + 2, 4))
        across_units = pl.ds(pl.multiple_of(opposite[1] * units, units), units)
        across = remote(
            w_in, whole_in.at[:, own_units], sends, receives, 4 * (feats - 1) + 2, opposite
        )
        beside = remote(
            w_in, whole_in.at[:, own_units], sends, receives, 4 * (feats - 1) + 3, partner
        )
        again = remote(
            whole_in.at[:, across_units],
            whole_in.at[:, across_units],
            sends,
            receives,
            4 * (feats - 1) + 4,
            partner,
        )
        across.start()
        beside.start()
    for peer in peers:
        their_rows = pl.ds(pl.multiple_of(peer[1] * share, share), share)
        if not relayed:
            copies.append(remote(w_in, whole_in.at[:, own_units], sends, receives, number, peer))
        copies.append(
            remote(bond.at[their_rows], rows.at[:, own_width], sends, receives, number + 1, peer)
        )
        copies.append(remote(w_down, whole_down.at[:, own_units], sends, receives, number + 2, peer))
        number += 3
    late.append(
        remote(state, state_window.at[:, 2 * atoms :], sends, receives, number, lower)
    )
    late.append(
        remote(state, state_window.at[:, :atoms], sends, receives, number + 1, upper)
    )
    number += 2
    for copy in copies + late:
        copy.start()
    own_rows = pl.ds(pl.multiple_of(feat * share, share), share)
    rows[:, own_width] = bond[own_rows]
    whole_in[:, own_units] = w_in[...]
    whole_down[:, own_units] = w_down[...]
    state_window[:, atoms : 2 * atoms] = state[...]
    if relayed:
        across.wait()
        again.start()
        copies = [beside, again] + copies
    for copy in copies:
        copy.wait()
    hidden[...] = silu(
        jnp.dot(rows[...], whole_in[...], preferred_element_type=jnp.float32)
    ).astype(jnp.bfloat16)
    sums = lax.dot_general(
        whole_down[...], hidden[...], (((1,), (1,)), ((), ())), preferred_element_type=jnp.float32
    )
    for part in range(share // block_size):
        limit = fill[feat * (share // block_size) + part]
        place = lax.broadcasted_iota(jnp.int32, (1, block_size), 1)
        mask = jnp.where(place < limit, 1.0, 0.0)
        span = slice(part * block_size, (part + 1) * block_size)
        angular_rows[:, span] = (sums[:, span] * mask).astype(jnp.bfloat16)
    own_span = pl.ds(pl.multiple_of(feat * share, share), share)
    back = []
    for peer in peers:
        theirs = pl.ds(pl.multiple_of(peer[1] * own_channels, own_channels), own_channels)
        back.append(
            remote(
                angular_rows.at[theirs], angular.at[:, own_span], sends, receives, number, peer
            )
        )
        number += 1
    for copy in back:
        copy.start()
    mine = pl.ds(pl.multiple_of(feat * own_channels, own_channels), own_channels)
    angular[:, own_span] = angular_rows[mine]
    for copy in back + late:
        copy.wait()


def pair_kernel(steps, blocks, source, owner, target, angular, coefficients, outgoing, total):
    step = pl.program_id(0)
    count = coefficients.shape[0]
    block_size = coefficients.shape[1]
    group = 14 if count % 14 == 0 else 1

    @pl.when(step == 0)
    def clear():
        total[...] = jnp.zeros_like(total)

    def several(turn, carry):
        products = []
        for offset in range(group):
            place = turn * group + offset
            start = pl.multiple_of(source[step * count + place] * block_size, block_size)
            products.append(
                lax.dot_general(
                    angular[:, pl.ds(start, block_size)],
                    coefficients[place],
                    (((1,), (1,)), ((), ())),
                    preferred_element_type=jnp.float32,
                )
            )
        for offset in range(group):
            pair = step * count + turn * group + offset
            slot = owner[pair] * blocks + target[pair]
            total[slot] += products[offset]
        return carry

    lax.fori_loop(0, count // group, several, 0)

    @pl.when(step == steps - 1)
    def finish():
        outgoing[...] = total[...].astype(jnp.bfloat16)


def update_kernel(
    spaces,
    feats,
    fill,
    outgoing,
    hidden_rows,
    state_window,
    bond,
    ends,
    w_gate,
    w_atom_in,
    w_atom,
    w_left,
    w_right,
    bond_out,
    atom_out,
    incoming,
    left_hot,
    right_hot,
    summed,
    message,
    halo_out,
    halo_in,
    mean,
    means,
    states,
    whole_atom_in,
    whole_atom,
    hidden,
    window_atoms,
    table,
    space_sends,
    space_receives,
    sends,
    receives,
):
    space, feat = lax.axis_index("space"), lax.axis_index("feat")
    blocks = fill.shape[0]
    slots = bond.shape[0]
    size = slots // blocks
    channels = summed.shape[0] // 2
    width = bond.shape[1]
    share = slots // feats
    window = state_window.shape[1]
    atoms = window // 3
    inner = w_atom.shape[0]
    peers = feat_peers(feats)
    lower, upper = down(space, -1), down(space, 1)
    sides = [(lower, feat), (upper, feat)]
    diagonal = [(side, peer[1]) for side in (lower, upper) for peer in peers]
    far = [(down(space, step), feat) for step in range(2, spaces - 1)]
    greet(peers + sides + diagonal + far)
    crossing = []
    for step in range(1, spaces):
        goal = down(space, step)
        crossing.append(
            remote(
                outgoing.at[pl.ds(goal * blocks, blocks)],
                incoming.at[space],
                space_sends,
                space_receives,
                step,
                (goal, feat),
            )
        )
    for copy in crossing:
        copy.start()
    own_inner = pl.ds(pl.multiple_of(feat * inner, inner), inner)
    own_span = pl.ds(pl.multiple_of(feat * share, share), share)
    weights, returned = [], []
    number = 0
    for peer in peers:
        theirs = pl.ds(pl.multiple_of(peer[1] * width, width), width)
        weights.append(
            remote(w_atom_in, whole_atom_in.at[feat], sends, receives, number, peer)
        )
        weights.append(remote(w_atom, whole_atom.at[own_inner], sends, receives, number + 1, peer))
        weights.append(
            remote(state_window, states.at[own_inner], sends, receives, number + 2, peer)
        )
        returned.append(
            remote(
                hidden_rows.at[:, theirs], hidden.at[own_span], sends, receives, number + 3, peer
            )
        )
        number += 4
    for copy in weights + returned:
        copy.start()
    incoming[space] = outgoing[pl.ds(space * blocks, blocks)]
    whole_atom_in[feat] = w_atom_in[...]
    whole_atom[own_inner] = w_atom[...]
    states[own_inner] = state_window[...]
    hidden[own_span] = hidden_rows[:, pl.ds(pl.multiple_of(feat * width, width), width)]
    place = lax.broadcasted_iota(jnp.int16, (size, window), 1)
    one, zero = jnp.bfloat16(1), jnp.bfloat16(0)

    def spread(block, carry):
        span = pl.ds(pl.multiple_of(block * size, size), size)
        pair = ends[span].astype(jnp.int16)
        left_hot[span] = jnp.where(place == pair[:, 0:1], one, zero)
        right_hot[span] = jnp.where(place == pair[:, 1:2], one, zero)
        return carry

    lax.fori_loop(0, blocks, spread, 0)
    for copy in crossing:
        copy.wait()
    own_channels = pl.ds(pl.multiple_of(feat * channels, channels), channels)
    for block in range(blocks):
        span = slice(block * size, (block + 1) * size)
        total = incoming[0, block].astype(jnp.float32)
        for source in range(1, spaces):
            total = total + incoming[source, block].astype(jnp.float32)
        lane = lax.broadcasted_iota(jnp.int32, (channels, size), 1)
        mask = jnp.where(lane < fill[block], 1.0, 0.0)
        summed[:channels, span] = (total * mask).astype(jnp.bfloat16)
        summed[channels:, span] = mask.astype(jnp.bfloat16)
    message[own_channels] = summed[:channels]
    spreading = []
    for peer in peers:
        spreading.append(
            remote(
                summed.at[:channels], message.at[own_channels], sends, receives, number, peer
            )
        )
        number += 1
    partial = jnp.dot(summed[...], right_hot[...], preferred_element_type=jnp.float32)
    halo_out[0] = partial[:, :atoms]
    halo_out[1] = partial[:, 2 * atoms :]
    halos = [
        remote(halo_out.at[0], halo_in.at[0], sends, receives, number, sides[0]),
        remote(halo_out.at[1], halo_in.at[1], sends, receives, number + 1, sides[1]),
    ]
    number += 2
    for copy in halos:
        copy.start()
    for copy in halos:
        copy.wait()
    full = partial[:, atoms : 2 * atoms] + halo_in[0] + halo_in[1]
    mean[...] = (full[:channels] / jnp.maximum(full[channels:], 1.0)).astype(jnp.bfloat16)
    sharing = []
    for peer in peers:
        spot = means.at[own_channels, atoms : 2 * atoms]
        sharing.append(remote(mean, spot, sends, receives, number, peer))
        number += 1
    for near in range(feats):
        for side in range(2):
            peer = ((lower, upper)[side], lax.rem(feat + near, feats))
            columns = slice(2 * atoms, 3 * atoms) if side == 0 else slice(0, atoms)
            spot = means.at[own_channels, columns]
            sharing.append(remote(mean, spot, sends, receives, number, peer))
            number += 1
    for copy in sharing + spreading:
        copy.start()
    means[own_channels, atoms : 2 * atoms] = mean[...]
    for copy in sharing + weights:
        copy.wait()
    first = (((0,), (0,)), ((), ()))
    mean_in = jnp.concatenate(
        [
            lax.dot_general(
                whole_atom_in[near], means[...], first, preferred_element_type=jnp.float32
            ).astype(jnp.bfloat16)
            for near in range(feats)
        ],
        axis=0,
    )
    pre = lax.dot_general(whole_atom[...], mean_in, first, preferred_element_type=jnp.float32)
    window_atoms[...] = (states[...].astype(jnp.float32) + silu(pre)).astype(jnp.bfloat16)
    atom_out[...] = window_atoms[own_inner, atoms : 2 * atoms]
    for copy in spreading + returned:
        copy.wait()
    table[...] = window_atoms[...].T
    row = lax.broadcasted_iota(jnp.int32, (size, width), 0)
    grouped = 4 if blocks % 4 == 0 else 1
    piece = grouped * size

    def finish(turn, carry):
        span = pl.ds(pl.multiple_of(turn * piece, piece), piece)
        left = jnp.dot(
            left_hot[span], table[...], preferred_element_type=jnp.float32
        ).astype(jnp.bfloat16)
        right = jnp.dot(
            right_hot[span], table[...], preferred_element_type=jnp.float32
        ).astype(jnp.bfloat16)
        mixed = jnp.dot(left, w_left[...], preferred_element_type=jnp.float32) + jnp.dot(
            right, w_right[...], preferred_element_type=jnp.float32
        )
        gate = lax.dot_general(
            message[:, span], w_gate[...], first, preferred_element_type=jnp.float32
        )
        update = (hidden[span].astype(jnp.float32) + silu(mixed)) / (1.0 + jnp.exp(-gate))
        old = bond[span].astype(jnp.float32)
        kept = [
            jnp.where(row < fill[turn * grouped + i], update[i * size : (i + 1) * size], 0.0)
            for i in range(grouped)
        ]
        bond_out[span] = (old + jnp.concatenate(kept, axis=0)).astype(jnp.bfloat16)
        return carry

    lax.fori_loop(0, blocks // grouped, finish, 0)


def fast(
    bond_state,
    block_fill,
    w_in,
    w_down,
    pair_coef,
    pair_source,
    pair_owner,
    pair_target,
    w_gate,
    w_atom_in,
    atom_state,
    w_atom,
    bond_ends,
    w_left,
    w_right,
):
    spaces, feats = lax.axis_size("space"), lax.axis_size("feat")
    slots, width = bond_state.shape
    blocks = block_fill.shape[0]
    size = slots // blocks
    pairs = pair_source.shape[0]
    features, units = w_in.shape
    channels = w_down.shape[1]
    own_channels = channels // feats
    share = slots // feats
    inner, atoms = atom_state.shape
    half, single = jnp.bfloat16, jnp.float32
    vmem = pl.BlockSpec(memory_space=pltpu.VMEM)
    smem = pl.BlockSpec(memory_space=pltpu.SMEM)
    dma = pltpu.SemaphoreType.DMA
    first_copies = 4 * (feats - 1) + 5
    angular, hidden_rows, state_window = pl.pallas_call(
        functools.partial(bond_kernel, feats),
        out_shape=(
            jax.ShapeDtypeStruct((own_channels, slots), half),
            jax.ShapeDtypeStruct((share, units * feats), half),
            jax.ShapeDtypeStruct((inner, 3 * atoms), half),
        ),
        in_specs=[smem] + [vmem] * 4,
        out_specs=(vmem, vmem, vmem),
        scratch_shapes=[
            pltpu.VMEM((share, features), half),
            pltpu.VMEM((features, units * feats), half),
            pltpu.VMEM((channels, features), half),
            pltpu.VMEM((channels, share), half),
            dma((first_copies,)),
            dma((first_copies,)),
        ],
        compiler_params=pltpu.CompilerParams(collective_id=0, has_side_effects=True),
        name="bond_mlp",
    )(block_fill, bond_state, w_in, w_down.T, atom_state)
    steps = 4 if pairs % 4 == 0 else 1
    part = pairs // steps
    outgoing = pl.pallas_call(
        functools.partial(pair_kernel, steps, blocks),
        grid=(steps,),
        out_shape=jax.ShapeDtypeStruct((spaces * blocks, own_channels, size), half),
        in_specs=[
            smem,
            smem,
            smem,
            pl.BlockSpec((own_channels, slots), lambda i: (0, 0)),
            pl.BlockSpec((part, size, size), lambda i: (i, 0, 0)),
        ],
        out_specs=pl.BlockSpec((spaces * blocks, own_channels, size), lambda i: (0, 0, 0)),
        scratch_shapes=[pltpu.VMEM((spaces * blocks, own_channels, size), single)],
        name="pair_sums",
    )(pair_source, pair_owner.reshape(pairs), pair_target, angular, pair_coef)
    last_copies = 4 * (feats - 1) + (feats - 1) + 2 + (feats - 1) + 2 * feats
    bond_out, atom_out = pl.pallas_call(
        functools.partial(update_kernel, spaces, feats),
        out_shape=(
            jax.ShapeDtypeStruct((slots, width), half),
            jax.ShapeDtypeStruct((inner, atoms), half),
        ),
        in_specs=[smem] + [vmem] * 10,
        out_specs=(vmem, vmem),
        scratch_shapes=[
            pltpu.VMEM((spaces, blocks, own_channels, size), half),
            pltpu.VMEM((slots, 3 * atoms), half),
            pltpu.VMEM((slots, 3 * atoms), half),
            pltpu.VMEM((2 * own_channels, slots), half),
            pltpu.VMEM((channels, slots), half),
            pltpu.VMEM((2, 2 * own_channels, atoms), single),
            pltpu.VMEM((2, 2 * own_channels, atoms), single),
            pltpu.VMEM((own_channels, atoms), half),
            pltpu.VMEM((channels, 3 * atoms), half),
            pltpu.VMEM((inner * feats, 3 * atoms), half),
            pltpu.VMEM((feats,) + w_atom_in.shape, half),
            pltpu.VMEM((inner * feats, w_atom.shape[1]), half),
            pltpu.VMEM((slots, width), half),
            pltpu.VMEM((inner * feats, 3 * atoms), half),
            pltpu.VMEM((3 * atoms, inner * feats), half),
            dma((spaces,)),
            dma((spaces,)),
            dma((last_copies,)),
            dma((last_copies,)),
        ],
        compiler_params=pltpu.CompilerParams(
            collective_id=1, has_side_effects=True, vmem_limit_bytes=60 * 2**20
        ),
        name="bond_update",
    )(
        block_fill,
        outgoing,
        hidden_rows,
        state_window,
        bond_state,
        bond_ends.T,
        w_gate,
        w_atom_in,
        w_atom,
        w_left,
        w_right,
    )
    return (bond_out, atom_out)


def solution(mesh):
    placed = (
        P("space", "feat"),
        P("space"),
        P(None, "feat"),
        P("feat", None),
        P("space", None, None),
        P("space"),
        P("space", None),
        P("space"),
        P(None, "feat"),
        P(None, "feat"),
        P("feat", "space"),
        P("feat", None),
        P(None, "space"),
        P(None, "feat"),
        P(None, "feat"),
    )
    spaces = mesh.shape["space"]
    body = fast if 4 <= spaces <= 16 else local
    return jax.shard_map(
        body,
        mesh=mesh,
        in_specs=placed,
        out_specs=(P("space", "feat"), P("feat", "space")),
        check_vma=False,
    )
```

```python
import functools

import jax
import jax.numpy as jnp
from jax import lax
from jax.experimental import pallas as pl
from jax.experimental.pallas import tpu as pltpu
from jax.sharding import PartitionSpec as P


def passed_along(value, axis, steps):
    count = lax.axis_size(axis)
    pairs = [(source, (source + steps) % count) for source in range(count)]
    return lax.ppermute(value, axis, pairs)


def extended(cells, sides, width):
    for axis, dim in sides:
        count = lax.axis_size(axis)
        head = lax.slice_in_dim(cells, 0, width, axis=dim)
        tail = lax.slice_in_dim(cells, cells.shape[dim] - width, cells.shape[dim], axis=dim)
        cells = jnp.concatenate(
            [
                lax.ppermute(tail, axis, [(i, (i + 1) % count) for i in range(count)]),
                cells,
                lax.ppermute(head, axis, [((i + 1) % count, i) for i in range(count)]),
            ],
            axis=dim,
        )
    return cells


def local(
    bond_state,
    block_fill,
    w_in,
    w_down,
    pair_coef,
    pair_source,
    pair_owner,
    pair_target,
    w_gate,
    w_atom_in,
    atom_state,
    w_atom,
    bond_ends,
    w_left,
    w_right,
):
    bond_slots = bond_state.shape[0]
    blocks = block_fill.shape[0]
    block_size = bond_slots // blocks
    pair_count = pair_source.shape[0]
    spaces = lax.axis_size("space")
    feat_count = lax.axis_size("feat")
    capacity = max(2, min(blocks, 2 * pair_count // spaces))
    channels = w_down.shape[1]
    own_channels = channels // feat_count
    atom_cols = atom_state.shape[1]
    contract_first = (((0,), (0,)), ((), ()))
    position = lax.broadcasted_iota(jnp.int32, (blocks, block_size), 1)
    real_mask = (position < block_fill[:, None]).astype(jnp.float32).reshape(bond_slots)
    full_rows = lax.all_gather(bond_state, "feat", axis=1, tiled=True)
    whole_in, whole_down = (
        lax.all_gather(w_in, "feat", axis=1, tiled=True),
        lax.all_gather(w_down, "feat", axis=0, tiled=True),
    )
    all_hidden = jax.nn.silu(
        jnp.dot(full_rows, whole_in, preferred_element_type=jnp.float32)
    ).astype(jnp.bfloat16)
    own_units = w_in.shape[1]
    hidden = lax.dynamic_slice_in_dim(all_hidden, lax.axis_index("feat") * own_units, own_units, 1)
    down_columns = lax.dynamic_slice_in_dim(
        whole_down, lax.axis_index("feat") * own_channels, own_channels, 1
    )
    angular_sum = lax.dot_general(
        down_columns, all_hidden, (((0,), (1,)), ((), ())), preferred_element_type=jnp.float32
    )
    angular = (angular_sum * real_mask[None, :]).astype(jnp.bfloat16)
    angular_blocks = angular.reshape(own_channels, blocks, block_size)
    sources = jnp.take(angular_blocks, pair_source, axis=1)
    contrib = jnp.einsum(
        "cpj,pij->pci", sources, pair_coef, preferred_element_type=jnp.float32
    ).astype(jnp.bfloat16)
    owner_ids = pair_owner[:, 0]
    owner_table = (
        owner_ids[:, None] == lax.broadcasted_iota(jnp.int32, (pair_count, spaces), 1)
    ).astype(jnp.int32)
    slot_rank = jnp.sum(jnp.cumsum(owner_table, axis=0) * owner_table, axis=1) - 1
    flat_slot = owner_ids * capacity + slot_rank
    outgoing = (
        jnp.zeros((spaces * capacity, own_channels, block_size), jnp.bfloat16)
        .at[flat_slot]
        .set(contrib)
    )
    labels = jnp.full((spaces * capacity,), blocks, jnp.int32).at[flat_slot].set(pair_target)
    incoming, arrived = (
        lax.all_to_all(
            outgoing.reshape(spaces, capacity, own_channels, block_size),
            "space",
            split_axis=0,
            concat_axis=0,
            tiled=True,
        ),
        lax.all_to_all(
            labels.reshape(spaces, capacity), "space", split_axis=0, concat_axis=0, tiled=True
        ),
    )
    chooser = (
        arrived.reshape(spaces * capacity)[None, :]
        == lax.broadcasted_iota(jnp.int32, (blocks, spaces * capacity), 0)
    ).astype(jnp.bfloat16)
    block_sums = jnp.einsum(
        "kq,qcr->ckr",
        chooser,
        incoming.reshape(spaces * capacity, own_channels, block_size),
        preferred_element_type=jnp.float32,
    )
    message = (block_sums.reshape(own_channels, bond_slots) * real_mask[None, :]).astype(
        jnp.bfloat16
    )
    shard_piece = lax.all_gather(message, "feat", axis=0, tiled=True)
    gate_pre = lax.dot_general(
        shard_piece, w_gate, contract_first, preferred_element_type=jnp.float32
    )
    to_atoms = lax.dot_general(
        shard_piece, w_atom_in, contract_first, preferred_element_type=jnp.float32
    )
    window = 3 * atom_cols
    window_sums = jax.ops.segment_sum(to_atoms, bond_ends[1], num_segments=window).T
    window_counts = jax.ops.segment_sum(real_mask, bond_ends[1], num_segments=window)
    from_upper = (
        passed_along(window_sums[:, :atom_cols].astype(jnp.bfloat16), "space", -1).astype(
            jnp.float32
        ),
        passed_along(window_counts[:atom_cols].astype(jnp.bfloat16), "space", -1).astype(
            jnp.float32
        ),
    )
    from_lower = (
        passed_along(window_sums[:, 2 * atom_cols :].astype(jnp.bfloat16), "space", 1).astype(
            jnp.float32
        ),
        passed_along(window_counts[2 * atom_cols :].astype(jnp.bfloat16), "space", 1).astype(
            jnp.float32
        ),
    )
    atom_sums = window_sums[:, atom_cols : 2 * atom_cols] + from_upper[0] + from_lower[0]
    atom_counts = window_counts[atom_cols : 2 * atom_cols] + from_upper[1] + from_lower[1]
    mean_in = (atom_sums / jnp.maximum(atom_counts, 1.0)[None, :]).astype(jnp.bfloat16)
    partial_pre = lax.dot_general(
        w_atom, mean_in, contract_first, preferred_element_type=jnp.float32
    )
    own_pre = lax.psum_scatter(
        partial_pre.astype(jnp.bfloat16), "feat", scatter_dimension=0, tiled=True
    ).astype(jnp.float32)
    atom_out = (atom_state + jax.nn.silu(own_pre)).astype(jnp.bfloat16)
    own_window = extended(atom_out, (("space", 1),), atom_cols)
    neighbours = lax.all_gather(own_window, "feat", axis=0, tiled=True)
    left_rows = jnp.take(neighbours, bond_ends[0], axis=1)
    right_rows = jnp.take(neighbours, bond_ends[1], axis=1)
    mixed_atoms = lax.dot_general(
        left_rows, w_left, contract_first, preferred_element_type=jnp.float32
    ) + lax.dot_general(right_rows, w_right, contract_first, preferred_element_type=jnp.float32)
    update = jax.nn.sigmoid(gate_pre) * (hidden.astype(jnp.float32) + jax.nn.silu(mixed_atoms))
    bond_out = (bond_state + real_mask[:, None] * update).astype(jnp.bfloat16)
    return (bond_out, atom_out)


MESH_IDS = pl.DeviceIdType.MESH


def silu(value):
    return value / (1.0 + jnp.exp(-value))


def greet(peers):
    barrier = pltpu.get_barrier_semaphore()
    for peer in peers:
        pl.semaphore_signal(barrier, inc=1, device_id=peer, device_id_type=MESH_IDS)
    pl.semaphore_wait(barrier, len(peers))


def remote(source, target, sends, receives, number, peer):
    return pltpu.make_async_remote_copy(
        src_ref=source,
        dst_ref=target,
        send_sem=sends.at[number],
        recv_sem=receives.at[number],
        device_id=peer,
        device_id_type=MESH_IDS,
    )


def feat_peers(count):
    space, feat = lax.axis_index("space"), lax.axis_index("feat")
    return [(space, lax.rem(feat + step, count)) for step in range(1, count)]


def down(value, step):
    count = lax.axis_size("space")
    return lax.rem(value + step + count, count)


def bond_kernel(
    feats,
    fill,
    bond,
    w_in,
    w_down,
    state,
    angular,
    hidden,
    state_window,
    rows,
    whole_in,
    whole_down,
    angular_rows,
    sends,
    receives,
):
    space, feat = lax.axis_index("space"), lax.axis_index("feat")
    share = bond.shape[0] // feats
    width, units = bond.shape[1], w_in.shape[1]
    own_channels = angular.shape[0]
    atoms = state.shape[1]
    block_size = bond.shape[0] // fill.shape[0]
    peers = feat_peers(feats)
    lower, upper = (down(space, -1), feat), (down(space, 1), feat)
    greet(peers + [lower, upper])
    own_width = pl.ds(pl.multiple_of(feat * width, width), width)
    own_units = pl.ds(pl.multiple_of(feat * units, units), units)
    copies, late = [], []
    number = 0
    relayed = feats == 4
    if relayed:
        partner = (space, feat + 1 - 2 * lax.rem(feat, 2))
        opposite = (space, lax.rem(feat + 2, 4))
        across_units = pl.ds(pl.multiple_of(opposite[1] * units, units), units)
        across = remote(
            w_in, whole_in.at[:, own_units], sends, receives, 4 * (feats - 1) + 2, opposite
        )
        beside = remote(
            w_in, whole_in.at[:, own_units], sends, receives, 4 * (feats - 1) + 3, partner
        )
        again = remote(
            whole_in.at[:, across_units],
            whole_in.at[:, across_units],
            sends,
            receives,
            4 * (feats - 1) + 4,
            partner,
        )
        across.start()
        beside.start()
    for peer in peers:
        their_rows = pl.ds(pl.multiple_of(peer[1] * share, share), share)
        if not relayed:
            copies.append(remote(w_in, whole_in.at[:, own_units], sends, receives, number, peer))
        copies.append(
            remote(bond.at[their_rows], rows.at[:, own_width], sends, receives, number + 1, peer)
        )
        copies.append(remote(w_down, whole_down.at[:, own_units], sends, receives, number + 2, peer))
        number += 3
    late.append(
        remote(state, state_window.at[:, 2 * atoms :], sends, receives, number, lower)
    )
    late.append(
        remote(state, state_window.at[:, :atoms], sends, receives, number + 1, upper)
    )
    number += 2
    for copy in copies + late:
        copy.start()
    own_rows = pl.ds(pl.multiple_of(feat * share, share), share)
    rows[:, own_width] = bond[own_rows]
    whole_in[:, own_units] = w_in[...]
    whole_down[:, own_units] = w_down[...]
    state_window[:, atoms : 2 * atoms] = state[...]
    if relayed:
        across.wait()
        again.start()
        copies = [beside, again] + copies
    for copy in copies:
        copy.wait()
    hidden[...] = silu(
        jnp.dot(rows[...], whole_in[...], preferred_element_type=jnp.float32)
    ).astype(jnp.bfloat16)
    sums = lax.dot_general(
        whole_down[...], hidden[...], (((1,), (1,)), ((), ())), preferred_element_type=jnp.float32
    )
    for part in range(share // block_size):
        limit = fill[feat * (share // block_size) + part]
        place = lax.broadcasted_iota(jnp.int32, (1, block_size), 1)
        mask = jnp.where(place < limit, 1.0, 0.0)
        span = slice(part * block_size, (part + 1) * block_size)
        angular_rows[:, span] = (sums[:, span] * mask).astype(jnp.bfloat16)
    own_span = pl.ds(pl.multiple_of(feat * share, share), share)
    back = []
    for peer in peers:
        theirs = pl.ds(pl.multiple_of(peer[1] * own_channels, own_channels), own_channels)
        back.append(
            remote(
                angular_rows.at[theirs], angular.at[:, own_span], sends, receives, number, peer
            )
        )
        number += 1
    for copy in back:
        copy.start()
    mine = pl.ds(pl.multiple_of(feat * own_channels, own_channels), own_channels)
    angular[:, own_span] = angular_rows[mine]
    for copy in back + late:
        copy.wait()


def pair_kernel(steps, blocks, source, owner, target, angular, coefficients, outgoing, total):
    step = pl.program_id(0)
    count = coefficients.shape[0]
    block_size = coefficients.shape[1]
    group = 14 if count % 14 == 0 else 1

    @pl.when(step == 0)
    def clear():
        total[...] = jnp.zeros_like(total)

    def several(turn, carry):
        products = []
        for offset in range(group):
            place = turn * group + offset
            start = pl.multiple_of(source[step * count + place] * block_size, block_size)
            products.append(
                lax.dot_general(
                    angular[:, pl.ds(start, block_size)],
                    coefficients[place],
                    (((1,), (1,)), ((), ())),
                    preferred_element_type=jnp.float32,
                )
            )
        for offset in range(group):
            pair = step * count + turn * group + offset
            slot = owner[pair] * blocks + target[pair]
            total[slot] += products[offset]
        return carry

    lax.fori_loop(0, count // group, several, 0)

    @pl.when(step == steps - 1)
    def finish():
        outgoing[...] = total[...].astype(jnp.bfloat16)


def update_kernel(
    spaces,
    feats,
    fill,
    outgoing,
    hidden_rows,
    state_window,
    bond,
    ends,
    w_gate,
    w_atom_in,
    w_atom,
    w_left,
    w_right,
    bond_out,
    atom_out,
    first_in,
    middle,
    incoming,
    left_hot,
    right_hot,
    summed,
    message,
    halo_out,
    halo_in,
    mean,
    means,
    states,
    whole_atom_in,
    whole_atom,
    hidden,
    window_atoms,
    table,
    space_sends,
    space_receives,
    sends,
    receives,
):
    space, feat = lax.axis_index("space"), lax.axis_index("feat")
    blocks = fill.shape[0]
    slots = bond.shape[0]
    size = slots // blocks
    channels = summed.shape[0] // 2
    width = bond.shape[1]
    share = slots // feats
    window = state_window.shape[1]
    atoms = window // 3
    inner = w_atom.shape[0]
    peers = feat_peers(feats)
    lower, upper = down(space, -1), down(space, 1)
    sides = [(lower, feat), (upper, feat)]
    diagonal = [(side, peer[1]) for side in (lower, upper) for peer in peers]
    half_count = spaces // 2
    parity = lax.rem(space, 2)
    partner = (space + 1 - 2 * parity, feat)
    order = sorted(range(1, half_count), key=lambda k: -min(k, half_count - k)) + [0]
    far = [(down(space, 2 * step), feat) for step in range(1, half_count)]
    greet(peers + sides + diagonal + far)
    paired, crossing = {}, []
    for step in order:
        goal = down(space, 2 * step) + 1 - 2 * parity
        paired[step] = remote(
            outgoing.at[pl.ds(goal * blocks, blocks)],
            first_in.at[step],
            space_sends,
            space_receives,
            step,
            partner,
        )
        paired[step].start()
    own_inner = pl.ds(pl.multiple_of(feat * inner, inner), inner)
    own_span = pl.ds(pl.multiple_of(feat * share, share), share)
    weights, returned = [], []
    number = 0
    for peer in peers:
        theirs = pl.ds(pl.multiple_of(peer[1] * width, width), width)
        weights.append(
            remote(w_atom_in, whole_atom_in.at[feat], sends, receives, number, peer)
        )
        weights.append(remote(w_atom, whole_atom.at[own_inner], sends, receives, number + 1, peer))
        weights.append(
            remote(state_window, states.at[own_inner], sends, receives, number + 2, peer)
        )
        returned.append(
            remote(
                hidden_rows.at[:, theirs], hidden.at[own_span], sends, receives, number + 3, peer
            )
        )
        number += 4
    for copy in weights + returned:
        copy.start()
    for step in order:
        goal = down(space, 2 * step)
        paired[step].wait()
        both = outgoing[pl.ds(goal * blocks, blocks)].astype(jnp.float32) + first_in[
            step
        ].astype(jnp.float32)
        place_of = incoming if step == 0 else middle
        place_of[step] = both.astype(jnp.bfloat16)
        if step:
            crossing.append(
                remote(
                    middle.at[step],
                    incoming.at[step],
                    space_sends,
                    space_receives,
                    half_count + step,
                    (goal, feat),
                )
            )
            crossing[-1].start()
    whole_atom_in[feat] = w_atom_in[...]
    whole_atom[own_inner] = w_atom[...]
    states[own_inner] = state_window[...]
    hidden[own_span] = hidden_rows[:, pl.ds(pl.multiple_of(feat * width, width), width)]
    place = lax.broadcasted_iota(jnp.int16, (size, window), 1)
    one, zero = jnp.bfloat16(1), jnp.bfloat16(0)

    def spread(block, carry):
        span = pl.ds(pl.multiple_of(block * size, size), size)
        pair = ends[:, span].T.astype(jnp.int16)
        left_hot[span] = jnp.where(place == pair[:, 0:1], one, zero)
        right_hot[span] = jnp.where(place == pair[:, 1:2], one, zero)
        return carry

    lax.fori_loop(0, blocks, spread, 0)
    for copy in crossing:
        copy.wait()
    own_channels = pl.ds(pl.multiple_of(feat * channels, channels), channels)
    for block in range(blocks):
        span = slice(block * size, (block + 1) * size)
        total = incoming[0, block].astype(jnp.float32)
        for source in range(1, half_count):
            total = total + incoming[source, block].astype(jnp.float32)
        lane = lax.broadcasted_iota(jnp.int32, (channels, size), 1)
        mask = jnp.where(lane < fill[block], 1.0, 0.0)
        summed[:channels, span] = (total * mask).astype(jnp.bfloat16)
        summed[channels:, span] = mask.astype(jnp.bfloat16)
    message[own_channels] = summed[:channels]
    spreading = []
    for peer in peers:
        spreading.append(
            remote(
                summed.at[:channels], message.at[own_channels], sends, receives, number, peer
            )
        )
        number += 1
    partial = jnp.dot(summed[...], right_hot[...], preferred_element_type=jnp.float32)
    halo_out[0] = partial[:, :atoms]
    halo_out[1] = partial[:, 2 * atoms :]
    halos = [
        remote(halo_out.at[0], halo_in.at[0], sends, receives, number, sides[0]),
        remote(halo_out.at[1], halo_in.at[1], sends, receives, number + 1, sides[1]),
    ]
    number += 2
    for copy in halos:
        copy.start()
    for copy in halos:
        copy.wait()
    full = partial[:, atoms : 2 * atoms] + halo_in[0] + halo_in[1]
    mean[...] = (full[:channels] / jnp.maximum(full[channels:], 1.0)).astype(jnp.bfloat16)
    sharing = []
    for peer in peers:
        spot = means.at[own_channels, atoms : 2 * atoms]
        sharing.append(remote(mean, spot, sends, receives, number, peer))
        number += 1
    for near in range(feats):
        for side in range(2):
            peer = ((lower, upper)[side], lax.rem(feat + near, feats))
            columns = slice(2 * atoms, 3 * atoms) if side == 0 else slice(0, atoms)
            spot = means.at[own_channels, columns]
            sharing.append(remote(mean, spot, sends, receives, number, peer))
            number += 1
    for copy in sharing + spreading:
        copy.start()
    means[own_channels, atoms : 2 * atoms] = mean[...]
    for copy in sharing + weights:
        copy.wait()
    first = (((0,), (0,)), ((), ()))
    mean_in = jnp.concatenate(
        [
            lax.dot_general(
                whole_atom_in[near], means[...], first, preferred_element_type=jnp.float32
            ).astype(jnp.bfloat16)
            for near in range(feats)
        ],
        axis=0,
    )
    pre = lax.dot_general(whole_atom[...], mean_in, first, preferred_element_type=jnp.float32)
    window_atoms[...] = (states[...].astype(jnp.float32) + silu(pre)).astype(jnp.bfloat16)
    atom_out[...] = window_atoms[own_inner, atoms : 2 * atoms]
    for copy in spreading + returned:
        copy.wait()
    table[...] = window_atoms[...].T
    row = lax.broadcasted_iota(jnp.int32, (size, width), 0)
    grouped = 4 if blocks % 4 == 0 else 1
    piece = grouped * size

    def finish(turn, carry):
        span = pl.ds(pl.multiple_of(turn * piece, piece), piece)
        left = jnp.dot(
            left_hot[span], table[...], preferred_element_type=jnp.float32
        ).astype(jnp.bfloat16)
        right = jnp.dot(
            right_hot[span], table[...], preferred_element_type=jnp.float32
        ).astype(jnp.bfloat16)
        mixed = jnp.dot(left, w_left[...], preferred_element_type=jnp.float32) + jnp.dot(
            right, w_right[...], preferred_element_type=jnp.float32
        )
        gate = lax.dot_general(
            message[:, span], w_gate[...], first, preferred_element_type=jnp.float32
        )
        update = (hidden[span].astype(jnp.float32) + silu(mixed)) / (1.0 + jnp.exp(-gate))
        old = bond[span].astype(jnp.float32)
        kept = [
            jnp.where(row < fill[turn * grouped + i], update[i * size : (i + 1) * size], 0.0)
            for i in range(grouped)
        ]
        bond_out[span] = (old + jnp.concatenate(kept, axis=0)).astype(jnp.bfloat16)
        return carry

    lax.fori_loop(0, blocks // grouped, finish, 0)


def fast(
    bond_state,
    block_fill,
    w_in,
    w_down,
    pair_coef,
    pair_source,
    pair_owner,
    pair_target,
    w_gate,
    w_atom_in,
    atom_state,
    w_atom,
    bond_ends,
    w_left,
    w_right,
):
    spaces, feats = lax.axis_size("space"), lax.axis_size("feat")
    slots, width = bond_state.shape
    blocks = block_fill.shape[0]
    size = slots // blocks
    pairs = pair_source.shape[0]
    features, units = w_in.shape
    channels = w_down.shape[1]
    own_channels = channels // feats
    share = slots // feats
    inner, atoms = atom_state.shape
    half, single = jnp.bfloat16, jnp.float32
    vmem = pl.BlockSpec(memory_space=pltpu.VMEM)
    smem = pl.BlockSpec(memory_space=pltpu.SMEM)
    dma = pltpu.SemaphoreType.DMA
    first_copies = 4 * (feats - 1) + 5
    angular, hidden_rows, state_window = pl.pallas_call(
        functools.partial(bond_kernel, feats),
        out_shape=(
            jax.ShapeDtypeStruct((own_channels, slots), half),
            jax.ShapeDtypeStruct((share, units * feats), half),
            jax.ShapeDtypeStruct((inner, 3 * atoms), half),
        ),
        in_specs=[smem] + [vmem] * 4,
        out_specs=(vmem, vmem, vmem),
        scratch_shapes=[
            pltpu.VMEM((share, features), half),
            pltpu.VMEM((features, units * feats), half),
            pltpu.VMEM((channels, features), half),
            pltpu.VMEM((channels, share), half),
            dma((first_copies,)),
            dma((first_copies,)),
        ],
        compiler_params=pltpu.CompilerParams(collective_id=0, has_side_effects=True),
        name="bond_mlp",
    )(block_fill, bond_state, w_in, w_down.T, atom_state)
    steps = 4 if pairs % 4 == 0 else 1
    part = pairs // steps
    outgoing = pl.pallas_call(
        functools.partial(pair_kernel, steps, blocks),
        grid=(steps,),
        out_shape=jax.ShapeDtypeStruct((spaces * blocks, own_channels, size), half),
        in_specs=[
            smem,
            smem,
            smem,
            pl.BlockSpec((own_channels, slots), lambda i: (0, 0)),
            pl.BlockSpec((part, size, size), lambda i: (i, 0, 0)),
        ],
        out_specs=pl.BlockSpec((spaces * blocks, own_channels, size), lambda i: (0, 0, 0)),
        scratch_shapes=[pltpu.VMEM((spaces * blocks, own_channels, size), single)],
        name="pair_sums",
    )(pair_source, pair_owner.reshape(pairs), pair_target, angular, pair_coef)
    last_copies = 4 * (feats - 1) + (feats - 1) + 2 + (feats - 1) + 2 * feats
    bond_out, atom_out = pl.pallas_call(
        functools.partial(update_kernel, spaces, feats),
        out_shape=(
            jax.ShapeDtypeStruct((slots, width), half),
            jax.ShapeDtypeStruct((inner, atoms), half),
        ),
        in_specs=[smem] + [vmem] * 10,
        out_specs=(vmem, vmem),
        scratch_shapes=[
            pltpu.VMEM((spaces // 2, blocks, own_channels, size), half),
            pltpu.VMEM((spaces // 2, blocks, own_channels, size), half),
            pltpu.VMEM((spaces // 2, blocks, own_channels, size), half),
            pltpu.VMEM((slots, 3 * atoms), half),
            pltpu.VMEM((slots, 3 * atoms), half),
            pltpu.VMEM((2 * own_channels, slots), half),
            pltpu.VMEM((channels, slots), half),
            pltpu.VMEM((2, 2 * own_channels, atoms), single),
            pltpu.VMEM((2, 2 * own_channels, atoms), single),
            pltpu.VMEM((own_channels, atoms), half),
            pltpu.VMEM((channels, 3 * atoms), half),
            pltpu.VMEM((inner * feats, 3 * atoms), half),
            pltpu.VMEM((feats,) + w_atom_in.shape, half),
            pltpu.VMEM((inner * feats, w_atom.shape[1]), half),
            pltpu.VMEM((slots, width), half),
            pltpu.VMEM((inner * feats, 3 * atoms), half),
            pltpu.VMEM((3 * atoms, inner * feats), half),
            dma((spaces,)),
            dma((spaces,)),
            dma((last_copies,)),
            dma((last_copies,)),
        ],
        compiler_params=pltpu.CompilerParams(
            collective_id=1, has_side_effects=True, vmem_limit_bytes=60 * 2**20
        ),
        name="bond_update",
    )(
        block_fill,
        outgoing,
        hidden_rows,
        state_window,
        bond_state,
        bond_ends,
        w_gate,
        w_atom_in,
        w_atom,
        w_left,
        w_right,
    )
    return (bond_out, atom_out)


def solution(mesh):
    placed = (
        P("space", "feat"),
        P("space"),
        P(None, "feat"),
        P("feat", None),
        P("space", None, None),
        P("space"),
        P("space", None),
        P("space"),
        P(None, "feat"),
        P(None, "feat"),
        P("feat", "space"),
        P("feat", None),
        P(None, "space"),
        P(None, "feat"),
        P(None, "feat"),
    )
    spaces = mesh.shape["space"]
    body = fast if spaces in range(4, 17, 2) else local
    return jax.shard_map(
        body,
        mesh=mesh,
        in_specs=placed,
        out_specs=(P("space", "feat"), P("feat", "space")),
        check_vma=False,
    )
```

```python
import functools

import jax
import jax.numpy as jnp
from jax import lax
from jax.experimental import pallas as pl
from jax.experimental.pallas import tpu as pltpu
from jax.sharding import PartitionSpec as P


def passed_along(value, axis, steps):
    count = lax.axis_size(axis)
    pairs = [(source, (source + steps) % count) for source in range(count)]
    return lax.ppermute(value, axis, pairs)


def extended(cells, sides, width):
    for axis, dim in sides:
        count = lax.axis_size(axis)
        head = lax.slice_in_dim(cells, 0, width, axis=dim)
        tail = lax.slice_in_dim(cells, cells.shape[dim] - width, cells.shape[dim], axis=dim)
        cells = jnp.concatenate(
            [
                lax.ppermute(tail, axis, [(i, (i + 1) % count) for i in range(count)]),
                cells,
                lax.ppermute(head, axis, [((i + 1) % count, i) for i in range(count)]),
            ],
            axis=dim,
        )
    return cells


def local(
    bond_state,
    block_fill,
    w_in,
    w_down,
    pair_coef,
    pair_source,
    pair_owner,
    pair_target,
    w_gate,
    w_atom_in,
    atom_state,
    w_atom,
    bond_ends,
    w_left,
    w_right,
):
    bond_slots = bond_state.shape[0]
    blocks = block_fill.shape[0]
    block_size = bond_slots // blocks
    pair_count = pair_source.shape[0]
    spaces = lax.axis_size("space")
    feat_count = lax.axis_size("feat")
    capacity = max(2, min(blocks, 2 * pair_count // spaces))
    channels = w_down.shape[1]
    own_channels = channels // feat_count
    atom_cols = atom_state.shape[1]
    contract_first = (((0,), (0,)), ((), ()))
    position = lax.broadcasted_iota(jnp.int32, (blocks, block_size), 1)
    real_mask = (position < block_fill[:, None]).astype(jnp.float32).reshape(bond_slots)
    full_rows = lax.all_gather(bond_state, "feat", axis=1, tiled=True)
    whole_in, whole_down = (
        lax.all_gather(w_in, "feat", axis=1, tiled=True),
        lax.all_gather(w_down, "feat", axis=0, tiled=True),
    )
    all_hidden = jax.nn.silu(
        jnp.dot(full_rows, whole_in, preferred_element_type=jnp.float32)
    ).astype(jnp.bfloat16)
    own_units = w_in.shape[1]
    hidden = lax.dynamic_slice_in_dim(all_hidden, lax.axis_index("feat") * own_units, own_units, 1)
    down_columns = lax.dynamic_slice_in_dim(
        whole_down, lax.axis_index("feat") * own_channels, own_channels, 1
    )
    angular_sum = lax.dot_general(
        down_columns, all_hidden, (((0,), (1,)), ((), ())), preferred_element_type=jnp.float32
    )
    angular = (angular_sum * real_mask[None, :]).astype(jnp.bfloat16)
    angular_blocks = angular.reshape(own_channels, blocks, block_size)
    sources = jnp.take(angular_blocks, pair_source, axis=1)
    contrib = jnp.einsum(
        "cpj,pij->pci", sources, pair_coef, preferred_element_type=jnp.float32
    ).astype(jnp.bfloat16)
    owner_ids = pair_owner[:, 0]
    owner_table = (
        owner_ids[:, None] == lax.broadcasted_iota(jnp.int32, (pair_count, spaces), 1)
    ).astype(jnp.int32)
    slot_rank = jnp.sum(jnp.cumsum(owner_table, axis=0) * owner_table, axis=1) - 1
    flat_slot = owner_ids * capacity + slot_rank
    outgoing = (
        jnp.zeros((spaces * capacity, own_channels, block_size), jnp.bfloat16)
        .at[flat_slot]
        .set(contrib)
    )
    labels = jnp.full((spaces * capacity,), blocks, jnp.int32).at[flat_slot].set(pair_target)
    incoming, arrived = (
        lax.all_to_all(
            outgoing.reshape(spaces, capacity, own_channels, block_size),
            "space",
            split_axis=0,
            concat_axis=0,
            tiled=True,
        ),
        lax.all_to_all(
            labels.reshape(spaces, capacity), "space", split_axis=0, concat_axis=0, tiled=True
        ),
    )
    chooser = (
        arrived.reshape(spaces * capacity)[None, :]
        == lax.broadcasted_iota(jnp.int32, (blocks, spaces * capacity), 0)
    ).astype(jnp.bfloat16)
    block_sums = jnp.einsum(
        "kq,qcr->ckr",
        chooser,
        incoming.reshape(spaces * capacity, own_channels, block_size),
        preferred_element_type=jnp.float32,
    )
    message = (block_sums.reshape(own_channels, bond_slots) * real_mask[None, :]).astype(
        jnp.bfloat16
    )
    shard_piece = lax.all_gather(message, "feat", axis=0, tiled=True)
    gate_pre = lax.dot_general(
        shard_piece, w_gate, contract_first, preferred_element_type=jnp.float32
    )
    to_atoms = lax.dot_general(
        shard_piece, w_atom_in, contract_first, preferred_element_type=jnp.float32
    )
    window = 3 * atom_cols
    window_sums = jax.ops.segment_sum(to_atoms, bond_ends[1], num_segments=window).T
    window_counts = jax.ops.segment_sum(real_mask, bond_ends[1], num_segments=window)
    from_upper = (
        passed_along(window_sums[:, :atom_cols].astype(jnp.bfloat16), "space", -1).astype(
            jnp.float32
        ),
        passed_along(window_counts[:atom_cols].astype(jnp.bfloat16), "space", -1).astype(
            jnp.float32
        ),
    )
    from_lower = (
        passed_along(window_sums[:, 2 * atom_cols :].astype(jnp.bfloat16), "space", 1).astype(
            jnp.float32
        ),
        passed_along(window_counts[2 * atom_cols :].astype(jnp.bfloat16), "space", 1).astype(
            jnp.float32
        ),
    )
    atom_sums = window_sums[:, atom_cols : 2 * atom_cols] + from_upper[0] + from_lower[0]
    atom_counts = window_counts[atom_cols : 2 * atom_cols] + from_upper[1] + from_lower[1]
    mean_in = (atom_sums / jnp.maximum(atom_counts, 1.0)[None, :]).astype(jnp.bfloat16)
    partial_pre = lax.dot_general(
        w_atom, mean_in, contract_first, preferred_element_type=jnp.float32
    )
    own_pre = lax.psum_scatter(
        partial_pre.astype(jnp.bfloat16), "feat", scatter_dimension=0, tiled=True
    ).astype(jnp.float32)
    atom_out = (atom_state + jax.nn.silu(own_pre)).astype(jnp.bfloat16)
    own_window = extended(atom_out, (("space", 1),), atom_cols)
    neighbours = lax.all_gather(own_window, "feat", axis=0, tiled=True)
    left_rows = jnp.take(neighbours, bond_ends[0], axis=1)
    right_rows = jnp.take(neighbours, bond_ends[1], axis=1)
    mixed_atoms = lax.dot_general(
        left_rows, w_left, contract_first, preferred_element_type=jnp.float32
    ) + lax.dot_general(right_rows, w_right, contract_first, preferred_element_type=jnp.float32)
    update = jax.nn.sigmoid(gate_pre) * (hidden.astype(jnp.float32) + jax.nn.silu(mixed_atoms))
    bond_out = (bond_state + real_mask[:, None] * update).astype(jnp.bfloat16)
    return (bond_out, atom_out)


MESH_IDS = pl.DeviceIdType.MESH


def silu(value):
    return value / (1.0 + jnp.exp(-value))


def greet(peers):
    barrier = pltpu.get_barrier_semaphore()
    for peer in peers:
        pl.semaphore_signal(barrier, inc=1, device_id=peer, device_id_type=MESH_IDS)
    pl.semaphore_wait(barrier, len(peers))


def remote(source, target, sends, receives, number, peer):
    return pltpu.make_async_remote_copy(
        src_ref=source,
        dst_ref=target,
        send_sem=sends.at[number],
        recv_sem=receives.at[number],
        device_id=peer,
        device_id_type=MESH_IDS,
    )


def feat_peers(count):
    space, feat = lax.axis_index("space"), lax.axis_index("feat")
    return [(space, lax.rem(feat + step, count)) for step in range(1, count)]


def down(value, step):
    count = lax.axis_size("space")
    return lax.rem(value + step + count, count)


def bond_kernel(
    feats,
    fill,
    bond,
    w_in,
    w_down,
    state,
    angular,
    hidden,
    state_window,
    rows,
    whole_in,
    whole_down,
    angular_rows,
    sends,
    receives,
):
    space, feat = lax.axis_index("space"), lax.axis_index("feat")
    share = bond.shape[0] // feats
    width, units = bond.shape[1], w_in.shape[1]
    own_channels = angular.shape[0]
    atoms = state.shape[1]
    block_size = bond.shape[0] // fill.shape[0]
    peers = feat_peers(feats)
    lower, upper = (down(space, -1), feat), (down(space, 1), feat)
    greet(peers + [lower, upper])
    own_width = pl.ds(pl.multiple_of(feat * width, width), width)
    own_units = pl.ds(pl.multiple_of(feat * units, units), units)
    copies, late = [], []
    number = 0
    relayed = feats == 4
    if relayed:
        partner = (space, feat + 1 - 2 * lax.rem(feat, 2))
        opposite = (space, lax.rem(feat + 2, 4))
        across_units = pl.ds(pl.multiple_of(opposite[1] * units, units), units)
        across = remote(
            w_in, whole_in.at[:, own_units], sends, receives, 4 * (feats - 1) + 2, opposite
        )
        beside = remote(
            w_in, whole_in.at[:, own_units], sends, receives, 4 * (feats - 1) + 3, partner
        )
        again = remote(
            whole_in.at[:, across_units],
            whole_in.at[:, across_units],
            sends,
            receives,
            4 * (feats - 1) + 4,
            partner,
        )
        across.start()
        beside.start()
    for peer in peers:
        their_rows = pl.ds(pl.multiple_of(peer[1] * share, share), share)
        if not relayed:
            copies.append(remote(w_in, whole_in.at[:, own_units], sends, receives, number, peer))
        copies.append(
            remote(bond.at[their_rows], rows.at[:, own_width], sends, receives, number + 1, peer)
        )
        copies.append(remote(w_down, whole_down.at[:, own_units], sends, receives, number + 2, peer))
        number += 3
    late.append(
        remote(state, state_window.at[:, 2 * atoms :], sends, receives, number, lower)
    )
    late.append(
        remote(state, state_window.at[:, :atoms], sends, receives, number + 1, upper)
    )
    number += 2
    for copy in copies + late:
        copy.start()
    own_rows = pl.ds(pl.multiple_of(feat * share, share), share)
    rows[:, own_width] = bond[own_rows]
    whole_in[:, own_units] = w_in[...]
    whole_down[:, own_units] = w_down[...]
    state_window[:, atoms : 2 * atoms] = state[...]
    if relayed:
        across.wait()
        again.start()
        copies = [beside, again] + copies
    for copy in copies:
        copy.wait()
    hidden[...] = silu(
        jnp.dot(rows[...], whole_in[...], preferred_element_type=jnp.float32)
    ).astype(jnp.bfloat16)
    sums = lax.dot_general(
        whole_down[...], hidden[...], (((1,), (1,)), ((), ())), preferred_element_type=jnp.float32
    )
    for part in range(share // block_size):
        limit = fill[feat * (share // block_size) + part]
        place = lax.broadcasted_iota(jnp.int32, (1, block_size), 1)
        mask = jnp.where(place < limit, 1.0, 0.0)
        span = slice(part * block_size, (part + 1) * block_size)
        angular_rows[:, span] = (sums[:, span] * mask).astype(jnp.bfloat16)
    own_span = pl.ds(pl.multiple_of(feat * share, share), share)
    back = []
    for peer in peers:
        theirs = pl.ds(pl.multiple_of(peer[1] * own_channels, own_channels), own_channels)
        back.append(
            remote(
                angular_rows.at[theirs], angular.at[:, own_span], sends, receives, number, peer
            )
        )
        number += 1
    for copy in back:
        copy.start()
    mine = pl.ds(pl.multiple_of(feat * own_channels, own_channels), own_channels)
    angular[:, own_span] = angular_rows[mine]
    for copy in back + late:
        copy.wait()


def pair_kernel(steps, blocks, source, owner, target, angular, coefficients, outgoing, total):
    step = pl.program_id(0)
    count = coefficients.shape[0]
    block_size = coefficients.shape[1]
    group = 28 if count % 28 == 0 else 1

    @pl.when(step == 0)
    def clear():
        total[...] = jnp.zeros_like(total)

    def several(turn, carry):
        products = []
        for offset in range(group):
            place = turn * group + offset
            start = pl.multiple_of(source[step * count + place] * block_size, block_size)
            products.append(
                lax.dot_general(
                    angular[:, pl.ds(start, block_size)],
                    coefficients[place],
                    (((1,), (1,)), ((), ())),
                    preferred_element_type=jnp.float32,
                )
            )
        for offset in range(group):
            pair = step * count + turn * group + offset
            slot = owner[pair] * blocks + target[pair]
            total[slot] += products[offset]
        return carry

    lax.fori_loop(0, count // group, several, 0)

    @pl.when(step == steps - 1)
    def finish():
        outgoing[...] = total[...].astype(jnp.bfloat16)


def update_kernel(
    spaces,
    feats,
    fill,
    outgoing,
    hidden_rows,
    state_window,
    bond,
    ends,
    w_gate,
    w_atom_in,
    w_atom,
    w_left,
    w_right,
    bond_out,
    atom_out,
    first_in,
    middle,
    incoming,
    left_hot,
    right_hot,
    summed,
    message,
    halo_out,
    halo_in,
    mean,
    means,
    states,
    whole_atom_in,
    whole_atom,
    hidden,
    window_atoms,
    table,
    space_sends,
    space_receives,
    sends,
    receives,
):
    space, feat = lax.axis_index("space"), lax.axis_index("feat")
    blocks = fill.shape[0]
    slots = bond.shape[0]
    size = slots // blocks
    channels = summed.shape[0] // 2
    width = bond.shape[1]
    share = slots // feats
    window = state_window.shape[1]
    atoms = window // 3
    inner = w_atom.shape[0]
    peers = feat_peers(feats)
    lower, upper = down(space, -1), down(space, 1)
    sides = [(lower, feat), (upper, feat)]
    diagonal = [(side, peer[1]) for side in (lower, upper) for peer in peers]
    half_count = spaces // 2
    parity = lax.rem(space, 2)
    partner = (space + 1 - 2 * parity, feat)
    order = sorted(range(1, half_count), key=lambda k: -min(k, half_count - k)) + [0]
    far = [(down(space, 2 * step), feat) for step in range(1, half_count)]
    greet(peers + sides + diagonal + far)
    paired, crossing = {}, []
    for step in order:
        goal = down(space, 2 * step) + 1 - 2 * parity
        paired[step] = remote(
            outgoing.at[pl.ds(goal * blocks, blocks)],
            first_in.at[step],
            space_sends,
            space_receives,
            step,
            partner,
        )
        paired[step].start()
    own_inner = pl.ds(pl.multiple_of(feat * inner, inner), inner)
    own_span = pl.ds(pl.multiple_of(feat * share, share), share)
    weights, returned = [], []
    number = 0
    for peer in peers:
        theirs = pl.ds(pl.multiple_of(peer[1] * width, width), width)
        weights.append(
            remote(w_atom_in, whole_atom_in.at[feat], sends, receives, number, peer)
        )
        weights.append(remote(w_atom, whole_atom.at[own_inner], sends, receives, number + 1, peer))
        weights.append(
            remote(state_window, states.at[own_inner], sends, receives, number + 2, peer)
        )
        returned.append(
            remote(
                hidden_rows.at[:, theirs], hidden.at[own_span], sends, receives, number + 3, peer
            )
        )
        number += 4
    for copy in weights + returned:
        copy.start()
    for step in order:
        goal = down(space, 2 * step)
        paired[step].wait()
        both = outgoing[pl.ds(goal * blocks, blocks)].astype(jnp.float32) + first_in[
            step
        ].astype(jnp.float32)
        place_of = incoming if step == 0 else middle
        place_of[step] = both.astype(jnp.bfloat16)
        if step:
            crossing.append(
                remote(
                    middle.at[step],
                    incoming.at[step],
                    space_sends,
                    space_receives,
                    half_count + step,
                    (goal, feat),
                )
            )
            crossing[-1].start()
    whole_atom_in[feat] = w_atom_in[...]
    whole_atom[own_inner] = w_atom[...]
    states[own_inner] = state_window[...]
    hidden[own_span] = hidden_rows[:, pl.ds(pl.multiple_of(feat * width, width), width)]
    place = lax.broadcasted_iota(jnp.int16, (size, window), 1)
    one, zero = jnp.bfloat16(1), jnp.bfloat16(0)

    def spread(block, carry):
        span = pl.ds(pl.multiple_of(block * size, size), size)
        pair = ends[:, span].T.astype(jnp.int16)
        left_hot[span] = jnp.where(place == pair[:, 0:1], one, zero)
        right_hot[span] = jnp.where(place == pair[:, 1:2], one, zero)
        return carry

    lax.fori_loop(0, blocks, spread, 0)
    for copy in crossing:
        copy.wait()
    own_channels = pl.ds(pl.multiple_of(feat * channels, channels), channels)
    for block in range(blocks):
        span = slice(block * size, (block + 1) * size)
        total = incoming[0, block].astype(jnp.float32)
        for source in range(1, half_count):
            total = total + incoming[source, block].astype(jnp.float32)
        lane = lax.broadcasted_iota(jnp.int32, (channels, size), 1)
        mask = jnp.where(lane < fill[block], 1.0, 0.0)
        summed[:channels, span] = (total * mask).astype(jnp.bfloat16)
        summed[channels:, span] = mask.astype(jnp.bfloat16)
    message[own_channels] = summed[:channels]
    spreading = []
    for peer in peers:
        spreading.append(
            remote(
                summed.at[:channels], message.at[own_channels], sends, receives, number, peer
            )
        )
        number += 1
    partial = jnp.dot(summed[...], right_hot[...], preferred_element_type=jnp.float32)
    halo_out[0] = partial[:, :atoms]
    halo_out[1] = partial[:, 2 * atoms :]
    halos = [
        remote(halo_out.at[0], halo_in.at[0], sends, receives, number, sides[0]),
        remote(halo_out.at[1], halo_in.at[1], sends, receives, number + 1, sides[1]),
    ]
    number += 2
    for copy in halos:
        copy.start()
    for copy in halos:
        copy.wait()
    full = partial[:, atoms : 2 * atoms] + halo_in[0] + halo_in[1]
    mean[...] = (full[:channels] / jnp.maximum(full[channels:], 1.0)).astype(jnp.bfloat16)
    sharing = []
    for peer in peers:
        spot = means.at[own_channels, atoms : 2 * atoms]
        sharing.append(remote(mean, spot, sends, receives, number, peer))
        number += 1
    for near in range(feats):
        for side in range(2):
            peer = ((lower, upper)[side], lax.rem(feat + near, feats))
            columns = slice(2 * atoms, 3 * atoms) if side == 0 else slice(0, atoms)
            spot = means.at[own_channels, columns]
            sharing.append(remote(mean, spot, sends, receives, number, peer))
            number += 1
    for copy in sharing + spreading:
        copy.start()
    means[own_channels, atoms : 2 * atoms] = mean[...]
    for copy in sharing + weights:
        copy.wait()
    first = (((0,), (0,)), ((), ()))
    mean_in = jnp.concatenate(
        [
            lax.dot_general(
                whole_atom_in[near], means[...], first, preferred_element_type=jnp.float32
            ).astype(jnp.bfloat16)
            for near in range(feats)
        ],
        axis=0,
    )
    pre = lax.dot_general(whole_atom[...], mean_in, first, preferred_element_type=jnp.float32)
    window_atoms[...] = (states[...].astype(jnp.float32) + silu(pre)).astype(jnp.bfloat16)
    atom_out[...] = window_atoms[own_inner, atoms : 2 * atoms]
    for copy in spreading + returned:
        copy.wait()
    table[...] = window_atoms[...].T
    row = lax.broadcasted_iota(jnp.int32, (size, width), 0)
    grouped = 4 if blocks % 4 == 0 else 1
    piece = grouped * size

    def finish(turn, carry):
        span = pl.ds(pl.multiple_of(turn * piece, piece), piece)
        left = jnp.dot(
            left_hot[span], table[...], preferred_element_type=jnp.float32
        ).astype(jnp.bfloat16)
        right = jnp.dot(
            right_hot[span], table[...], preferred_element_type=jnp.float32
        ).astype(jnp.bfloat16)
        mixed = jnp.dot(left, w_left[...], preferred_element_type=jnp.float32) + jnp.dot(
            right, w_right[...], preferred_element_type=jnp.float32
        )
        gate = lax.dot_general(
            message[:, span], w_gate[...], first, preferred_element_type=jnp.float32
        )
        update = (hidden[span].astype(jnp.float32) + silu(mixed)) / (1.0 + jnp.exp(-gate))
        old = bond[span].astype(jnp.float32)
        kept = [
            jnp.where(row < fill[turn * grouped + i], update[i * size : (i + 1) * size], 0.0)
            for i in range(grouped)
        ]
        bond_out[span] = (old + jnp.concatenate(kept, axis=0)).astype(jnp.bfloat16)
        return carry

    lax.fori_loop(0, blocks // grouped, finish, 0)


def fast(
    bond_state,
    block_fill,
    w_in,
    w_down,
    pair_coef,
    pair_source,
    pair_owner,
    pair_target,
    w_gate,
    w_atom_in,
    atom_state,
    w_atom,
    bond_ends,
    w_left,
    w_right,
):
    spaces, feats = lax.axis_size("space"), lax.axis_size("feat")
    slots, width = bond_state.shape
    blocks = block_fill.shape[0]
    size = slots // blocks
    pairs = pair_source.shape[0]
    features, units = w_in.shape
    channels = w_down.shape[1]
    own_channels = channels // feats
    share = slots // feats
    inner, atoms = atom_state.shape
    half, single = jnp.bfloat16, jnp.float32
    vmem = pl.BlockSpec(memory_space=pltpu.VMEM)
    smem = pl.BlockSpec(memory_space=pltpu.SMEM)
    dma = pltpu.SemaphoreType.DMA
    first_copies = 4 * (feats - 1) + 5
    angular, hidden_rows, state_window = pl.pallas_call(
        functools.partial(bond_kernel, feats),
        out_shape=(
            jax.ShapeDtypeStruct((own_channels, slots), half),
            jax.ShapeDtypeStruct((share, units * feats), half),
            jax.ShapeDtypeStruct((inner, 3 * atoms), half),
        ),
        in_specs=[smem] + [vmem] * 4,
        out_specs=(vmem, vmem, vmem),
        scratch_shapes=[
            pltpu.VMEM((share, features), half),
            pltpu.VMEM((features, units * feats), half),
            pltpu.VMEM((channels, features), half),
            pltpu.VMEM((channels, share), half),
            dma((first_copies,)),
            dma((first_copies,)),
        ],
        compiler_params=pltpu.CompilerParams(collective_id=0, has_side_effects=True),
        name="bond_mlp",
    )(block_fill, bond_state, w_in, w_down.T, atom_state)
    steps = 4 if pairs % 4 == 0 else 1
    part = pairs // steps
    outgoing = pl.pallas_call(
        functools.partial(pair_kernel, steps, blocks),
        grid=(steps,),
        out_shape=jax.ShapeDtypeStruct((spaces * blocks, own_channels, size), half),
        in_specs=[
            smem,
            smem,
            smem,
            pl.BlockSpec((own_channels, slots), lambda i: (0, 0)),
            pl.BlockSpec((part, size, size), lambda i: (i, 0, 0)),
        ],
        out_specs=pl.BlockSpec((spaces * blocks, own_channels, size), lambda i: (0, 0, 0)),
        scratch_shapes=[pltpu.VMEM((spaces * blocks, own_channels, size), single)],
        name="pair_sums",
    )(pair_source, pair_owner.reshape(pairs), pair_target, angular, pair_coef)
    last_copies = 4 * (feats - 1) + (feats - 1) + 2 + (feats - 1) + 2 * feats
    bond_out, atom_out = pl.pallas_call(
        functools.partial(update_kernel, spaces, feats),
        out_shape=(
            jax.ShapeDtypeStruct((slots, width), half),
            jax.ShapeDtypeStruct((inner, atoms), half),
        ),
        in_specs=[smem] + [vmem] * 10,
        out_specs=(vmem, vmem),
        scratch_shapes=[
            pltpu.VMEM((spaces // 2, blocks, own_channels, size), half),
            pltpu.VMEM((spaces // 2, blocks, own_channels, size), half),
            pltpu.VMEM((spaces // 2, blocks, own_channels, size), half),
            pltpu.VMEM((slots, 3 * atoms), half),
            pltpu.VMEM((slots, 3 * atoms), half),
            pltpu.VMEM((2 * own_channels, slots), half),
            pltpu.VMEM((channels, slots), half),
            pltpu.VMEM((2, 2 * own_channels, atoms), single),
            pltpu.VMEM((2, 2 * own_channels, atoms), single),
            pltpu.VMEM((own_channels, atoms), half),
            pltpu.VMEM((channels, 3 * atoms), half),
            pltpu.VMEM((inner * feats, 3 * atoms), half),
            pltpu.VMEM((feats,) + w_atom_in.shape, half),
            pltpu.VMEM((inner * feats, w_atom.shape[1]), half),
            pltpu.VMEM((slots, width), half),
            pltpu.VMEM((inner * feats, 3 * atoms), half),
            pltpu.VMEM((3 * atoms, inner * feats), half),
            dma((spaces,)),
            dma((spaces,)),
            dma((last_copies,)),
            dma((last_copies,)),
        ],
        compiler_params=pltpu.CompilerParams(
            collective_id=1, has_side_effects=True, vmem_limit_bytes=60 * 2**20
        ),
        name="bond_update",
    )(
        block_fill,
        outgoing,
        hidden_rows,
        state_window,
        bond_state,
        bond_ends,
        w_gate,
        w_atom_in,
        w_atom,
        w_left,
        w_right,
    )
    return (bond_out, atom_out)


def solution(mesh):
    placed = (
        P("space", "feat"),
        P("space"),
        P(None, "feat"),
        P("feat", None),
        P("space", None, None),
        P("space"),
        P("space", None),
        P("space"),
        P(None, "feat"),
        P(None, "feat"),
        P("feat", "space"),
        P("feat", None),
        P(None, "space"),
        P(None, "feat"),
        P(None, "feat"),
    )
    spaces = mesh.shape["space"]
    body = fast if spaces in range(4, 17, 2) else local
    return jax.shard_map(
        body,
        mesh=mesh,
        in_specs=placed,
        out_specs=(P("space", "feat"), P("feat", "space")),
        check_vma=False,
    )
```
